128 devices in a mesh: own: 16 (over y, z), red: 8 (over x, core).
Axes of the slice: x: 4, y: 4, z: 4, core: 2. Of those that a mesh axis runs over, the one named last changes fastest.
Arguments:
- amp_tiles: bfloat16 [8192, 128, 128], P(('own', 'red')), may hold values from -6 to 6
- int_tiles: bfloat16 [8192, 128, 128], P(('own', 'red')), may hold values from -0.0625 to 0.0625
- requests: int32 [16, 8, 16, 2, 8], P('own', 'red'), may hold values from -1 to 63, as said below
- tri_amp: int32 [512, 8, 64], P('own', 'red'), may hold values from 0 to 127, as said below
- tri_int: int32 [512, 8, 64], P('own', 'red'), may hold values from 0 to 127, as said below
- tri_count: int32 [512, 8], P('own', 'red'), may hold values from 1 to 64, as said below
Outputs:
- residual: float32 [512, 128, 128], P(('own', 'red'))
The draws below stay inside these ranges and needn't reach their ends.
Inputs may be any that keep to these rules, and one draw needn't show every extreme that they name: -1 marks an empty slot and live slots come first; the live numbers in one row of 8 slots are distinct; every owner device has 8 live amplitude requests to some holder and 8 live integral requests to some holder. tri_amp[t, r, k] // 8 is a holder h and tri_amp[t, r, k] % 8 is below the number of live amplitude requests of the owner of t, on red index r, to h. `tri_int`: likewise for the integral requests. `tri_count`: on every owner and red index some residual tile has 64 live triples.
All inputs are finite; a program needn't handle non-finite values.
Results may differ from the reference program's by a relative error of at most 0.0003.
Values may be sent and summed in bfloat16 or wider, within the bound.
No kernel may reach another device: no remote copies, remote signals or barrier semaphores. Data moves between devices by JAX's collectives and lax.ppermute only.
A program may use at most 128 MiB of HBM per device.

```python
import math
import jax
import jax.numpy as jnp
from jax import lax

TILE = 128
OUT_TILES = 32
SLOTS = 64
CAP = 8
STORE = 64
STORED = 8192
N_OWN = 16
N_RED = 8


def request_plan(key):
    key_count = jax.random.fold_in(key, 11)
    key_full = jax.random.fold_in(key, 12)
    key_perm = jax.random.fold_in(key, 13)
    live_counts = jax.random.randint(key_count, (N_OWN, N_RED, N_OWN, 2), 2, CAP + 1)
    full_holder = jax.random.randint(key_full, (N_OWN, N_RED, 1, 2), 0, N_OWN)
    holder_iota = jnp.arange(N_OWN, dtype=jnp.int32)[None, None, :, None]
    live_counts = jnp.where((holder_iota == full_holder) | (holder_iota == N_OWN - 1), CAP, live_counts)
    perm_keys = jax.random.split(key_perm, N_OWN * N_RED * N_OWN * 2)
    chosen = jax.vmap(lambda single: jax.random.permutation(single, STORE)[:CAP])(perm_keys)
    chosen = chosen.reshape(N_OWN, N_RED, N_OWN, 2, CAP)
    slot_iota = jnp.arange(CAP, dtype=jnp.int32)
    wanted = jnp.where(slot_iota < live_counts[..., None], chosen, -1)
    return (wanted.astype(jnp.int32), live_counts)


def pick_positions(key, live_counts):
    holder = jax.random.randint(jax.random.fold_in(key, 1), (N_OWN, OUT_TILES, N_RED, SLOTS), 0, N_OWN)
    table = jnp.broadcast_to(live_counts[:, None, :, :], (N_OWN, OUT_TILES, N_RED, N_OWN))
    limit = jnp.take_along_axis(table, holder, axis=3)
    slot_pick = jax.random.randint(jax.random.fold_in(key, 2), holder.shape, 0, limit)
    values = holder * CAP + slot_pick
    values = values.at[0, 0, 0, 0].set(N_OWN * CAP - 1)
    values = values.at[0, 0, 0, 1].set(0)
    return values.reshape(N_OWN * OUT_TILES, N_RED, SLOTS).astype(jnp.int32)


def draw_requests(key, part):
    return request_plan(key)[0]


def draw_tri_amp(key, part):
    live_counts = request_plan(key)[1]
    return pick_positions(jax.random.fold_in(key, 21), live_counts[..., 0])


def draw_tri_int(key, part):
    live_counts = request_plan(key)[1]
    return pick_positions(jax.random.fold_in(key, 22), live_counts[..., 1])


def draw_tri_count(key, part):
    factor = jax.random.randint(jax.random.fold_in(key, 31), (N_OWN, 1, N_RED), 1, 5)
    base_count = jax.random.randint(jax.random.fold_in(key, 32), (N_OWN, OUT_TILES, N_RED), 1, SLOTS // 4 + 1)
    counts = jnp.minimum(base_count * factor, SLOTS)
    full_at = jax.random.randint(jax.random.fold_in(key, 33), (N_OWN, 1, N_RED), 0, OUT_TILES)
    tile_iota = jnp.arange(OUT_TILES, dtype=jnp.int32)[None, :, None]
    counts = jnp.where(tile_iota == full_at, SLOTS, counts)
    return counts.reshape(N_OWN * OUT_TILES, N_RED).astype(jnp.int32)


def level_of(rng, shape, cuts, low, high):
    factor_of = 1.0
    for dim, shards_of in cuts:
        draws = jax.random.uniform(jax.random.fold_in(jax.random.fold_in(rng, 6), dim), (shards_of,), jnp.float32, low / len(cuts), high / len(cuts))
        factor_of = factor_of * jnp.repeat(jnp.exp(draws), shape[dim] // shards_of).reshape((-1,) + (1,) * (len(shape) - 1 - dim))
    return factor_of


def scatter_about(rng, extent, width, bound, shards=(), kind=jnp.bfloat16):
    level = level_of(rng, extent, shards, -0.22, 0.18) if shards else 1.0
    values = jax.random.normal(rng, extent, jnp.float32) * width * level
    return jnp.minimum(jnp.maximum(values, -bound), bound).astype(kind)


def setup_inputs(seed: int = 0) -> dict:
    key_of = jax.random.split(jax.random.key(seed), 7)
    return {
        "amp_tiles": scatter_about(key_of[0], (STORED, TILE, TILE), 1.0, 6.0, ((0, 128),)),
        "int_tiles": scatter_about(key_of[1], (STORED, TILE, TILE), (TILE * SLOTS) ** -0.5, 0.0625, ((0, 128),)),
        "requests": draw_requests(jax.random.fold_in(key_of[6], 71), 0),
        "tri_amp": draw_tri_amp(jax.random.fold_in(key_of[6], 71), 0),
        "tri_int": draw_tri_int(jax.random.fold_in(key_of[6], 71), 0),
        "tri_count": draw_tri_count(jax.random.fold_in(key_of[6], 71), 0),
    }


def contract_rows(recv_amp, recv_int, amp_pos, int_pos, counts):
    row_count, slot_count = amp_pos.shape
    block_rows = math.gcd(8, row_count)
    keep_mask = jnp.arange(slot_count, dtype=jnp.int32)[None, :] < counts[:, None]

    def one_block(operands):
        block_amp, block_int, block_keep = operands
        left_tiles = jnp.where(block_keep[:, :, None, None], recv_amp[block_amp], 0).astype(jnp.float32)
        right_tiles = recv_int[block_int].astype(jnp.float32)
        return jnp.einsum("nkpc,nkqc->npq", left_tiles, right_tiles, precision=lax.Precision.HIGHEST)

    def in_blocks(values):
        return values.reshape((row_count // block_rows, block_rows) + values.shape[1:])

    product = lax.map(one_block, (in_blocks(amp_pos), in_blocks(int_pos), in_blocks(keep_mask)))
    return product.reshape(row_count, TILE, TILE)


def reference(amp_tiles, int_tiles, requests, tri_amp, tri_int, tri_count):
    store_amp = amp_tiles.reshape(N_OWN, N_RED, STORE, TILE, TILE)
    store_int = int_tiles.reshape(N_OWN, N_RED, STORE, TILE, TILE)
    holders = jnp.arange(N_OWN, dtype=jnp.int32)

    def receive(store, wanted, red_index):
        clipped = jnp.clip(wanted, 0, STORE - 1).astype(jnp.int32)
        picked = store[holders[:, None], red_index, clipped]
        picked = jnp.where((wanted >= 0)[:, :, None, None], picked, 0)
        return picked.reshape(N_OWN * CAP, TILE, TILE)

    def one_owner(owner):
        first_row = (owner * OUT_TILES).astype(jnp.int32)
        amp_rows = lax.dynamic_slice_in_dim(tri_amp, first_row, OUT_TILES, 0)
        int_rows = lax.dynamic_slice_in_dim(tri_int, first_row, OUT_TILES, 0)
        count_rows = lax.dynamic_slice_in_dim(tri_count, first_row, OUT_TILES, 0)

        def one_partner(total_sum, red_index):
            wanted = requests[owner, red_index]
            recv_amp = receive(store_amp, wanted[:, 0], red_index)
            recv_int = receive(store_int, wanted[:, 1], red_index)
            added = contract_rows(recv_amp, recv_int, amp_rows[:, red_index], int_rows[:, red_index], count_rows[:, red_index])
            return total_sum + added, None

        start_sum = jnp.zeros((OUT_TILES, TILE, TILE), jnp.float32)
        total_sum, unused = lax.scan(one_partner, start_sum, jnp.arange(N_RED, dtype=jnp.int32))
        return total_sum

    result = lax.map(one_owner, jnp.arange(N_OWN, dtype=jnp.int32))
    return result.reshape(N_OWN * OUT_TILES, TILE, TILE)
```

```python
import functools

import jax
import jax.numpy as jnp
from jax import lax
from jax.experimental import pallas as pl
from jax.experimental.pallas import tpu as pltpu
from jax.sharding import PartitionSpec as P

GROUP = 4


def pack_body(lists, asked, *refs):
    stores, out, sem = refs[:-2], refs[-2], refs[-1]
    peers, slots = out.shape[0], out.shape[1]
    cap = asked.shape[1] // 2
    last = stores[0].shape[0] - 1

    def one_peer(peer, carry):
        for pos, (which, kind, slot) in enumerate(lists):
            tile = jnp.clip(asked[peer, kind * cap + slot], 0, last)
            pltpu.make_async_copy(stores[which].at[tile], out.at[peer, pos], sem).start()
        return carry

    lax.fori_loop(0, peers, one_peer, 0)
    pltpu.make_async_copy(out, out, sem).wait()


def pack(lists, asked, stores):
    peers = asked.shape[0]
    tile = stores[0].shape[1:]
    return pl.pallas_call(
        functools.partial(pack_body, lists),
        in_specs=[pl.BlockSpec(memory_space=pltpu.SMEM)] + [pl.BlockSpec(memory_space=pl.ANY)] * len(stores),
        out_specs=pl.BlockSpec(memory_space=pl.ANY),
        out_shape=jax.ShapeDtypeStruct((peers, len(lists)) + tile, stores[0].dtype),
        scratch_shapes=[pltpu.SemaphoreType.DMA(())],
    )(asked, *stores)


def row_sum(row, start, stop, left_at, right_at, left_buf, right_buf, zero_slot, acc):
    groups = (stop - start + GROUP - 1) // GROUP

    def one_group(g, acc):
        base = start + g * GROUP
        lefts, rights = [], []
        for j in range(GROUP):
            pos = base + j
            left = jnp.where(pos < stop, left_at[row, pos], zero_slot)
            lefts.append(left_buf[left])
            rights.append(right_buf[right_at[row, pos]])
        return acc + lax.dot_general(
            jnp.concatenate(lefts, axis=1),
            jnp.concatenate(rights, axis=1),
            (((1,), (1,)), ((), ())),
            preferred_element_type=jnp.float32,
        )

    return lax.fori_loop(0, groups, one_group, acc)


def first_body(left_at, right_at, low, got, out, buf, sem):
    copy = pltpu.make_async_copy(got, buf.at[pl.ds(0, got.shape[0])], sem)
    copy.start()
    zero_slot = got.shape[0]
    buf[zero_slot] = jnp.zeros(buf.shape[1:], buf.dtype)
    copy.wait()

    def one_row(row, carry):
        out[row] = row_sum(row, 0, low[row], left_at, right_at, buf, buf, zero_slot, jnp.zeros(out.shape[1:], out.dtype))
        return carry

    lax.fori_loop(0, out.shape[0], one_row, 0)


def second_body(left_at, right_at, low, live, place, got, rest, before, out, left_buf, right_buf, acc_buf, sems):
    holders, cap = left_buf.shape[0] - 1, left_buf.shape[1]
    copies = [
        pltpu.make_async_copy(before, acc_buf, sems.at[0]),
        pltpu.make_async_copy(got.at[:, pl.ds(0, cap)], left_buf.at[pl.ds(0, holders)], sems.at[1]),
        pltpu.make_async_copy(rest, right_buf, sems.at[2]),
    ]
    for copy in copies:
        copy.start()
    left_buf[holders, 0] = jnp.zeros(left_buf.shape[2:], left_buf.dtype)
    for copy in copies:
        copy.wait()
    flat_left = left_buf.reshape((holders + 1) * cap, left_buf.shape[2], left_buf.shape[3])
    zero_slot = holders * cap
    half, steps, share = out.shape[0], out.shape[1], out.shape[2]

    def one_out(i, carry):
        side = i // (steps * share)
        step = (i // share) % steps
        j = i % share
        core = jnp.where(side == 0, 1 - place[1], place[1])
        row = (((place[0] + step) % steps) * half + core) * share + j
        out[side, step, j] = row_sum(
            row, low[row], live[row], left_at, right_at, flat_left, right_buf, zero_slot, acc_buf[row]
        )
        return carry

    lax.fori_loop(0, half * steps * share, one_out, 0)


def body(amp_tiles, int_tiles, requests, tri_amp, tri_int, tri_count):
    wanted = requests[0, 0]
    peers, kinds, cap = wanted.shape
    rows, slots = tri_amp.shape[0], tri_amp.shape[2]
    tile = amp_tiles.shape[1:]
    cut = cap // 2
    red = lax.axis_size("red")
    share = rows // red
    me = lax.axis_index("red")

    asked = lax.all_to_all(wanted.reshape(peers, kinds * cap), "own", split_axis=0, concat_axis=0, tiled=True)
    first_list = tuple((0, 0, s) for s in range(cap)) + tuple((1, 1, s) for s in range(cut))
    second_list = tuple((0, 1, s) for s in range(cut, cap))
    send_first = pack(first_list, asked, (amp_tiles, int_tiles))
    got_first = lax.all_to_all(send_first, "own", split_axis=0, concat_axis=0, tiled=True)
    send_second = pack(second_list, asked, (int_tiles,))
    got_second = lax.all_to_all(send_second, "own", split_axis=0, concat_axis=0, tiled=True)

    amp_pos, int_pos = tri_amp[:, 0], tri_int[:, 0]
    count = tri_count[:, 0]
    alive = lax.broadcasted_iota(jnp.int32, (rows, slots), 1) < count[:, None]
    is_low = int_pos % cap < cut
    key = jnp.where(alive, jnp.where(is_low, 0, 1), 2)
    code = lax.sort((key * peers * cap + amp_pos) * peers * cap + int_pos, dimension=1)
    low = jnp.sum((alive & is_low).astype(jnp.int32), axis=1)
    amp_pos = (code // (peers * cap)) % (peers * cap)
    int_pos = code % (peers * cap)
    pad = ((0, 0), (0, GROUP))
    width = cap + cut
    holder, slot = int_pos // cap, int_pos % cap
    left_first = jnp.pad((amp_pos // cap) * width + amp_pos % cap, pad)
    right_first = jnp.pad(jnp.where(slot < cut, holder * width + cap + slot, 0), pad)
    left_second = jnp.pad(amp_pos, pad)
    right_second = jnp.pad(jnp.where(slot < cut, 0, holder * (cap - cut) + slot - cut), pad)

    smem = pl.BlockSpec(memory_space=pltpu.SMEM)
    anywhere = pl.BlockSpec(memory_space=pl.ANY)
    vmem = pl.BlockSpec(memory_space=pltpu.VMEM)
    params = pltpu.CompilerParams(vmem_limit_bytes=40 * 2**20)
    flat_first = got_first.reshape((-1,) + tile)
    before = pl.pallas_call(
        first_body,
        in_specs=[smem] * 3 + [anywhere],
        out_specs=vmem,
        out_shape=jax.ShapeDtypeStruct((rows,) + tile, jnp.float32),
        scratch_shapes=[pltpu.VMEM((flat_first.shape[0] + 1,) + tile, flat_first.dtype), pltpu.SemaphoreType.DMA(())],
        compiler_params=params,
    )(left_first, right_first, low, flat_first)

    place = jnp.stack([me // 2, me % 2]).astype(jnp.int32)
    flat_second = got_second.reshape((-1,) + tile)
    steps = red // 2
    part = pl.pallas_call(
        second_body,
        in_specs=[smem] * 5 + [anywhere] * 3,
        out_specs=vmem,
        out_shape=jax.ShapeDtypeStruct((2, steps, share) + tile, jnp.float32),
        scratch_shapes=[
            pltpu.VMEM((peers + 1, cap) + tile, flat_first.dtype),
            pltpu.VMEM(flat_second.shape, flat_second.dtype),
            pltpu.VMEM((rows,) + tile, jnp.float32),
            pltpu.SemaphoreType.DMA((3,)),
        ],
        compiler_params=params,
    )(left_second, right_second, low, count, place, got_first, flat_second, before)

    swapped = lax.ppermute(part[0], "red", [(i, i ^ 1) for i in range(red)])
    total = swapped[0] + part[1, 0]
    for step in [steps // 2] + [s for s in range(1, steps) if s != steps // 2]:
        block = swapped[step] + part[1, step]
        total = total + lax.ppermute(
            block, "red", [(i, ((i // 2 + step) % steps) * 2 + i % 2) for i in range(red)]
        )
    return total


def solution(mesh):
    placed = (
        P(("own", "red"), None, None),
        P(("own", "red"), None, None),
        P("own", "red", None, None, None),
        P("own", "red", None),
        P("own", "red", None),
        P("own", "red"),
    )
    return jax.shard_map(
        body, mesh=mesh, in_specs=placed, out_specs=P(("own", "red"), None, None), check_vma=False
    )
```

```python
import functools

import jax
import jax.numpy as jnp
from jax import lax
from jax.experimental import pallas as pl
from jax.experimental.pallas import tpu as pltpu
from jax.sharding import PartitionSpec as P

GROUP = 4
UNROLL = 4
PACK_STEPS = 4


def pack_body(lists, asked, *refs):
    stores, out = refs[:-1], refs[-1]
    cap = asked.shape[1] // 2
    last = stores[0].shape[0] - 1
    peers = out.shape[0]
    first = pl.program_id(0) * peers
    for peer in range(peers):
        for pos, (which, kind, slot) in enumerate(lists):
            tile = jnp.clip(asked[first + peer, kind * cap + slot], 0, last)
            out[peer, pos] = stores[which][tile]


def pack(lists, asked, stores):
    peers = asked.shape[0]
    tile = stores[0].shape[1:]
    steps = PACK_STEPS
    whole = pl.BlockSpec(stores[0].shape, lambda i: (0, 0, 0))
    return pl.pallas_call(
        functools.partial(pack_body, lists),
        grid=(steps,),
        in_specs=[pl.BlockSpec(memory_space=pltpu.SMEM)] + [whole] * len(stores),
        out_specs=pl.BlockSpec((peers // steps, len(lists)) + tile, lambda i: (i, 0, 0, 0)),
        out_shape=jax.ShapeDtypeStruct((peers, len(lists)) + tile, stores[0].dtype),
    )(asked, *stores)


def contract_groups(groups, left_at, right_at, table, left, right, out):
    zero_tile = left.shape[0] - 1

    def one_step(i, carry):
        sums = []
        for u in range(UNROLL):
            g = i * UNROLL + u
            row, base, stop = table[0, g], table[1, g], table[2, g]
            lefts, rights = [], []
            for j in range(GROUP):
                pos = base + j
                lefts.append(left[jnp.where(pos < stop, left_at[row, pos], zero_tile)])
                rights.append(right[right_at[row, pos]])
            sums.append(
                lax.dot_general(
                    jnp.concatenate(lefts, axis=1),
                    jnp.concatenate(rights, axis=1),
                    (((1,), (1,)), ((), ())),
                    preferred_element_type=jnp.float32,
                )
            )
        for u in range(UNROLL):
            place = table[3, i * UNROLL + u]
            out[place] = out[place] + sums[u]
        return carry

    lax.fori_loop(0, (groups[0] + UNROLL - 1) // UNROLL, one_step, 0)


def flatten(ref):
    return ref.reshape((ref.shape[0] * ref.shape[1],) + ref.shape[2:])


def first_body(groups, left_at, right_at, table, got, out, buf, sem):
    holders, width = got.shape[0], got.shape[1]
    copy = pltpu.make_async_copy(got, buf.at[pl.ds(0, holders)], sem)
    copy.start()
    buf[holders, width - 1] = jnp.zeros(buf.shape[2:], buf.dtype)
    out[...] = jnp.zeros(out.shape, out.dtype)
    copy.wait()
    flat = flatten(buf)
    contract_groups(groups, left_at, right_at, table, flat, flat, out)


def second_body(groups, left_at, right_at, table, got, rest, before, out, buf, rest_buf, sems):
    holders, width = got.shape[0], got.shape[1]
    cap = width - rest.shape[1]
    copies = [
        pltpu.make_async_copy(got.at[:, pl.ds(0, cap)], buf.at[pl.ds(0, holders), pl.ds(0, cap)], sems.at[0]),
        pltpu.make_async_copy(rest, rest_buf, sems.at[1]),
        pltpu.make_async_copy(before, out, sems.at[2]),
    ]
    for copy in copies:
        copy.start()
    buf[holders, width - 1] = jnp.zeros(buf.shape[2:], buf.dtype)
    for copy in copies:
        copy.wait()
    contract_groups(groups, left_at, right_at, table, flatten(buf), flatten(rest_buf), out)


def group_table(start, stop, places, slots):
    rows = start.shape[0]
    size = (stop - start + GROUP - 1) // GROUP
    end = jnp.sum(jnp.where(jnp.arange(rows)[:, None] >= jnp.arange(rows)[None, :], size[None, :], 0), axis=1)
    limit = rows * (slots // GROUP) + 2 * UNROLL
    number = jnp.arange(limit, dtype=jnp.int32)[:, None]
    passed = number >= end[None, :]
    row = jnp.minimum(jnp.sum(passed.astype(jnp.int32), axis=1), rows - 1)
    opened = jnp.max(jnp.where(passed, end[None, :], 0), axis=1)
    mine = row[:, None] == jnp.arange(rows)[None, :]

    def of_row(values):
        return jnp.sum(jnp.where(mine, values[None, :], 0), axis=1)

    base = of_row(start) + (number[:, 0] - opened) * GROUP
    base = jnp.where(number[:, 0] < end[-1], base, slots)
    return end[-1:], jnp.stack([row, base, of_row(stop), of_row(places)]).astype(jnp.int32)


def body(amp_tiles, int_tiles, requests, tri_amp, tri_int, tri_count):
    wanted = requests[0, 0]
    peers, kinds, cap = wanted.shape
    rows, slots = tri_amp.shape[0], tri_amp.shape[2]
    tile = amp_tiles.shape[1:]
    cut = cap // 2
    red = lax.axis_size("red")
    share = rows // red
    steps = red // 2
    me = lax.axis_index("red")

    asked = lax.all_to_all(wanted.reshape(peers, kinds * cap), "own", split_axis=0, concat_axis=0, tiled=True)
    first_list = tuple((0, 0, s) for s in range(cap)) + tuple((1, 1, s) for s in range(cut))
    second_list = tuple((0, 1, s) for s in range(cut, cap))
    send_first = pack(first_list, asked, (amp_tiles, int_tiles))
    got_first = lax.all_to_all(send_first, "own", split_axis=0, concat_axis=0, tiled=True)
    send_second = pack(second_list, asked, (int_tiles,))
    got_second = lax.all_to_all(send_second, "own", split_axis=0, concat_axis=0, tiled=True)

    amp_pos, int_pos = tri_amp[:, 0], tri_int[:, 0]
    count = tri_count[:, 0]
    alive = lax.broadcasted_iota(jnp.int32, (rows, slots), 1) < count[:, None]
    is_low = int_pos % cap < cut
    key = jnp.where(alive, jnp.where(is_low, 0, 1), 2)
    code = lax.sort((key * peers * cap + amp_pos) * peers * cap + int_pos, dimension=1)
    low = jnp.sum((alive & is_low).astype(jnp.int32), axis=1)
    amp_pos = (code // (peers * cap)) % (peers * cap)
    int_pos = code % (peers * cap)
    pad = ((0, 0), (0, GROUP))
    width = cap + cut
    holder, slot = int_pos // cap, int_pos % cap
    left_at = jnp.pad((amp_pos // cap) * width + amp_pos % cap, pad)
    right_at = jnp.where(slot < cut, holder * width + cap + slot, holder * (cap - cut) + slot - cut)
    right_at = jnp.pad(jnp.where(code < 2 * (peers * cap) ** 2, right_at, 0), pad)

    row = jnp.arange(rows, dtype=jnp.int32)
    side = jnp.where((row // share) % 2 == me % 2, 1, 0)
    step = (row // (2 * share) - me // 2) % steps
    places = (side * steps + step) * share + row % share
    first_groups, first_table = group_table(jnp.zeros_like(low), low, places, slots)
    second_groups, second_table = group_table(low, count, places, slots)

    smem = pl.BlockSpec(memory_space=pltpu.SMEM)
    vmem = pl.BlockSpec(memory_space=pltpu.VMEM)
    anywhere = pl.BlockSpec(memory_space=pl.ANY)
    result = jax.ShapeDtypeStruct((rows,) + tile, jnp.float32)
    buf = pltpu.VMEM((peers + 1, width) + tile, got_first.dtype)
    before = pl.pallas_call(
        first_body,
        in_specs=[smem] * 4 + [anywhere],
        out_specs=vmem,
        out_shape=result,
        scratch_shapes=[buf, pltpu.SemaphoreType.DMA(())],
    )(first_groups, left_at, right_at, first_table, got_first)
    part = pl.pallas_call(
        second_body,
        in_specs=[smem] * 4 + [anywhere] * 3,
        out_specs=vmem,
        out_shape=result,
        scratch_shapes=[buf, pltpu.VMEM(got_second.shape, got_second.dtype), pltpu.SemaphoreType.DMA((3,))],
    )(second_groups, left_at, right_at, second_table, got_first, got_second, before)
    part = part.reshape((2, steps, share) + tile)

    swapped = lax.ppermute(part[0], "red", [(i, i ^ 1) for i in range(red)])
    total = swapped[0] + part[1, 0]
    for step in [steps // 2] + [s for s in range(1, steps) if s != steps // 2]:
        block = swapped[step] + part[1, step]
        total = total + lax.ppermute(
            block, "red", [(i, ((i // 2 + step) % steps) * 2 + i % 2) for i in range(red)]
        )
    return total


def solution(mesh):
    placed = (
        P(("own", "red"), None, None),
        P(("own", "red"), None, None),
        P("own", "red", None, None, None),
        P("own", "red", None),
        P("own", "red", None),
        P("own", "red"),
    )
    return jax.shard_map(
        body, mesh=mesh, in_specs=placed, out_specs=P(("own", "red"), None, None), check_vma=False
    )
```

```python
import functools

import jax
import jax.numpy as jnp
from jax import lax
from jax.experimental import pallas as pl
from jax.experimental.pallas import tpu as pltpu
from jax.sharding import PartitionSpec as P

GROUP = 4
UNROLL = 4
PACK_STEPS = 4


def pack_body(lists, asked, *refs):
    stores, outs = refs[:2], refs[2:]
    cap = asked.shape[1] // 2
    last = stores[0].shape[0] - 1
    peers = outs[0].shape[0]
    first = pl.program_id(0) * peers
    for peer in range(peers):
        for out, picks in zip(outs, lists):
            for pos, (kind, slot) in enumerate(picks):
                tile = jnp.clip(asked[first + peer, kind * cap + slot], 0, last)
                out[peer, pos] = stores[kind][tile]


def pack(lists, asked, stores):
    peers = asked.shape[0]
    tile = stores[0].shape[1:]
    whole = pl.BlockSpec(stores[0].shape, lambda i: (0, 0, 0))
    return pl.pallas_call(
        functools.partial(pack_body, lists),
        grid=(PACK_STEPS,),
        in_specs=[pl.BlockSpec(memory_space=pltpu.SMEM), whole, whole],
        out_specs=[
            pl.BlockSpec((peers // PACK_STEPS, len(picks)) + tile, lambda i: (i, 0, 0, 0)) for picks in lists
        ],
        out_shape=[jax.ShapeDtypeStruct((peers, len(picks)) + tile, stores[0].dtype) for picks in lists],
    )(asked, *stores)


def group_dot(lefts, rights):
    return lax.dot_general(
        jnp.concatenate(lefts, axis=1),
        jnp.concatenate(rights, axis=1),
        (((1,), (1,)), ((), ())),
        preferred_element_type=jnp.float32,
    )


def contract(bounds, left_at, right_at, table, ends, left, right, acc, first, part):
    places = acc.shape[0]
    begin, finish = bounds[first // places], bounds[first // places + 1]

    def full_step(i, carry):
        sums = []
        for u in range(UNROLL):
            g = begin + i * UNROLL + u
            row, base = table[0, g], table[1, g]
            lefts = [left[left_at[row, base + j]] for j in range(GROUP)]
            rights = [right[right_at[row, base + j]] for j in range(GROUP)]
            sums.append(group_dot(lefts, rights))
        for u in range(UNROLL):
            g = begin + i * UNROLL + u
            place = jnp.minimum(table[2, g] - first, places - 1)
            acc[place] = acc[place] + jnp.where(g < finish, sums[u], 0.0)
        return carry

    lax.fori_loop(0, (finish - begin + UNROLL - 1) // UNROLL, full_step, 0)

    def rest_step(i, carry):
        sums = []
        for u in range(UNROLL):
            place = first + i * UNROLL + u
            row, stop = ends[0, place], ends[1, place]
            base = stop - ends[2, place] % GROUP
            lefts, rights = [], []
            for j in range(GROUP):
                tile = left[left_at[row, base + j]]
                lefts.append(jnp.where(base + j < stop, tile, jnp.zeros_like(tile)))
                rights.append(right[right_at[row, base + j]])
            sums.append(group_dot(lefts, rights))
        for u in range(UNROLL):
            place = i * UNROLL + u
            acc[place] = acc[place] + sums[u]
        return carry

    lax.fori_loop(0, places // UNROLL, rest_step, 0)


def flatten(ref):
    return ref.reshape((ref.shape[0] * ref.shape[1],) + ref.shape[2:])


def first_body(bounds, left_at, right_at, table, ends, got, out):
    out[...] = jnp.zeros(out.shape, out.dtype)
    flat = flatten(got)
    contract(bounds, left_at, right_at, table, ends, flat, flat, out, 0, 0)


def second_body(first, bounds, left_at, right_at, table, ends, got, rest, before, other, mine, acc):
    places = acc.shape[0]
    acc[...] = before[pl.ds(first, places)]
    contract(bounds, left_at, right_at, table, ends, flatten(got), flatten(rest), acc, first, 1)
    other[...] = acc[pl.ds(0, places // 2)]
    mine[...] = acc[pl.ds(places // 2, places // 2)]


def group_table(order, start, stop, slots):
    rows = start.shape[0]
    at = order[:, None] == jnp.arange(rows)[None, :]

    def in_order(values):
        return jnp.sum(jnp.where(at, values[None, :], 0), axis=1)

    start, stop = in_order(start), in_order(stop)
    size = (stop - start) // GROUP
    end = jnp.sum(jnp.where(jnp.arange(rows)[:, None] >= jnp.arange(rows)[None, :], size[None, :], 0), axis=1)
    limit = rows * (slots // GROUP) + 2 * UNROLL
    number = jnp.arange(limit, dtype=jnp.int32)[:, None]
    passed = number >= end[None, :]
    place = jnp.minimum(jnp.sum(passed.astype(jnp.int32), axis=1), rows - 1)
    opened = jnp.max(jnp.where(passed, end[None, :], 0), axis=1)
    mine = place[:, None] == jnp.arange(rows)[None, :]

    def of_place(values):
        return jnp.sum(jnp.where(mine, values[None, :], 0), axis=1)

    base = of_place(start) + (number[:, 0] - opened) * GROUP
    base = jnp.where(number[:, 0] < end[-1], base, slots)
    table = jnp.stack([of_place(order), base, place]).astype(jnp.int32)
    ends = jnp.stack([order, stop, stop - start]).astype(jnp.int32)
    return end.astype(jnp.int32), table, ends


def body(amp_tiles, int_tiles, requests, tri_amp, tri_int, tri_count):
    wanted = requests[0, 0]
    peers, kinds, cap = wanted.shape
    rows, slots = tri_amp.shape[0], tri_amp.shape[2]
    tile = amp_tiles.shape[1:]
    cut = cap // 2
    red = lax.axis_size("red")
    share = rows // red
    steps = red // 2
    me = lax.axis_index("red")

    wanted, me = lax.optimization_barrier((wanted, me))
    asked = lax.all_to_all(wanted.reshape(peers, kinds * cap), "own", split_axis=0, concat_axis=0, tiled=True)
    first_list = tuple((0, s) for s in range(cap)) + tuple((1, s) for s in range(cut))
    second_list = tuple((1, s) for s in range(cut, cap))
    asked, me = lax.optimization_barrier((asked, me))
    send_first, send_second = pack((first_list, second_list), asked, (amp_tiles, int_tiles))
    got_first = lax.all_to_all(send_first, "own", split_axis=0, concat_axis=0, tiled=True)
    got_first, send_second, tri_amp, tri_int, tri_count, me = lax.optimization_barrier(
        (got_first, send_second, tri_amp, tri_int, tri_count, me)
    )
    got_second = lax.all_to_all(send_second, "own", split_axis=0, concat_axis=0, tiled=True)

    amp_pos, int_pos = tri_amp[:, 0], tri_int[:, 0]
    count = tri_count[:, 0]
    alive = lax.broadcasted_iota(jnp.int32, (rows, slots), 1) < count[:, None]
    is_low = int_pos % cap < cut
    key = jnp.where(alive, jnp.where(is_low, 0, 1), 2)
    code = lax.sort((key * peers * cap + amp_pos) * peers * cap + int_pos, dimension=1)
    low = jnp.sum((alive & is_low).astype(jnp.int32), axis=1)
    amp_pos = (code // (peers * cap)) % (peers * cap)
    int_pos = code % (peers * cap)
    pad = ((0, 0), (0, GROUP))
    width = cap + cut
    holder, slot = int_pos // cap, int_pos % cap
    left_at = jnp.pad((amp_pos // cap) * width + amp_pos % cap, pad)
    right_at = jnp.where(slot < cut, holder * width + cap + slot, holder * (cap - cut) + slot - cut)
    right_at = jnp.pad(jnp.where(code < 2 * (peers * cap) ** 2, right_at, 0), pad)

    place = jnp.arange(rows, dtype=jnp.int32)
    step, side = place // (2 * share), (place // share) % 2
    order = (((me // 2 + step) % steps) * 2 + jnp.where(side == 0, 1 - me % 2, me % 2)) * share + place % share
    first_end, first_table, first_ends = group_table(order, jnp.zeros_like(low), low, slots)
    second_end, second_table, second_ends = group_table(order, low, count, slots)
    first_bounds = jnp.pad(first_end[rows - 1 :], (1, 0))
    second_bounds = jnp.pad(second_end[2 * share - 1 :: 2 * share], (1, 0))

    smem = pl.BlockSpec(memory_space=pltpu.SMEM)
    vmem = pl.BlockSpec(memory_space=pltpu.VMEM)
    params = pltpu.CompilerParams(vmem_limit_bytes=24 * 2**20)
    before = pl.pallas_call(
        first_body,
        in_specs=[smem] * 5 + [vmem],
        out_specs=vmem,
        out_shape=jax.ShapeDtypeStruct((rows,) + tile, jnp.float32),
        compiler_params=params,
    )(first_bounds, left_at, right_at, first_table, first_ends, got_first)

    def second(step):
        half = jax.ShapeDtypeStruct((share,) + tile, jnp.float32)
        return pl.pallas_call(
            functools.partial(second_body, step * 2 * share),
            in_specs=[smem] * 5 + [vmem] * 3,
            out_specs=[vmem, vmem],
            out_shape=[half, half],
            scratch_shapes=[pltpu.VMEM((2 * share,) + tile, jnp.float32)],
            compiler_params=params,
        )(second_bounds, left_at, right_at, second_table, second_ends, got_first, got_second, before)

    swap = [(i, i ^ 1) for i in range(red)]
    arrived = []
    for step in [steps // 2] + [s for s in range(1, steps) if s != steps // 2]:
        other, mine = second(step)
        block = mine + lax.ppermute(other, "red", swap)
        arrived.append(lax.ppermute(block, "red", [(i, ((i // 2 + step) % steps) * 2 + i % 2) for i in range(red)]))
    other, mine = second(0)
    total = mine + lax.ppermute(other, "red", swap)
    for block in arrived:
        total = total + block
    return total


def solution(mesh):
    placed = (
        P(("own", "red"), None, None),
        P(("own", "red"), None, None),
        P("own", "red", None, None, None),
        P("own", "red", None),
        P("own", "red", None),
        P("own", "red"),
    )
    return jax.shard_map(
        body, mesh=mesh, in_specs=placed, out_specs=P(("own", "red"), None, None), check_vma=False
    )
```

```python
import functools

import jax
import jax.numpy as jnp
from jax import lax
from jax.experimental import pallas as pl
from jax.experimental.pallas import tpu as pltpu
from jax.sharding import PartitionSpec as P

GROUP = 4
UNROLL = 4
PACK_STEPS = 4


def pack_body(lists, asked, *refs):
    stores, outs = refs[:2], refs[2:]
    cap = asked.shape[1] // 2
    last = stores[0].shape[0] - 1
    peers = outs[0].shape[0]
    first = pl.program_id(0) * peers
    for peer in range(peers):
        for out, picks in zip(outs, lists):
            for pos, (kind, slot) in enumerate(picks):
                tile = jnp.clip(asked[first + peer, kind * cap + slot], 0, last)
                out[peer, pos] = stores[kind][tile]


def pack(lists, asked, stores):
    peers = asked.shape[0]
    tile = stores[0].shape[1:]
    whole = pl.BlockSpec(stores[0].shape, lambda i: (0, 0, 0))
    return pl.pallas_call(
        functools.partial(pack_body, lists),
        grid=(PACK_STEPS,),
        in_specs=[pl.BlockSpec(memory_space=pltpu.SMEM), whole, whole],
        out_specs=[
            pl.BlockSpec((peers // PACK_STEPS, len(picks)) + tile, lambda i: (i, 0, 0, 0)) for picks in lists
        ],
        out_shape=[jax.ShapeDtypeStruct((peers, len(picks)) + tile, stores[0].dtype) for picks in lists],
    )(asked, *stores)


def group_dot(lefts, rights):
    return lax.dot_general(
        jnp.concatenate(lefts, axis=1),
        jnp.concatenate(rights, axis=1),
        (((1,), (1,)), ((), ())),
        preferred_element_type=jnp.float32,
    )


def contract(bounds, left_at, right_at, table, ends, left, right, acc, first):
    places = acc.shape[0]
    begin, finish = bounds[first // places], bounds[first // places + 1]

    def full_step(i, carry):
        sums = []
        for u in range(UNROLL):
            g = begin + i * UNROLL + u
            row, base = table[0, g], table[1, g]
            lefts = [left[left_at[row, base + j]] for j in range(GROUP)]
            rights = [right[right_at[row, base + j]] for j in range(GROUP)]
            sums.append(group_dot(lefts, rights))
        for u in range(UNROLL):
            g = begin + i * UNROLL + u
            place = jnp.minimum(table[2, g] - first, places - 1)
            acc[place] = acc[place] + jnp.where(g < finish, sums[u], 0.0)
        return carry

    lax.fori_loop(0, (finish - begin + UNROLL - 1) // UNROLL, full_step, 0)

    def rest_step(i, carry):
        sums = []
        for u in range(UNROLL):
            place = first + i * UNROLL + u
            row, stop = ends[0, place], ends[1, place]
            base = stop - ends[2, place] % GROUP
            lefts, rights = [], []
            for j in range(GROUP):
                tile = left[left_at[row, base + j]]
                lefts.append(jnp.where(base + j < stop, tile, jnp.zeros_like(tile)))
                rights.append(right[right_at[row, base + j]])
            sums.append(group_dot(lefts, rights))
        for u in range(UNROLL):
            place = i * UNROLL + u
            acc[place] = acc[place] + sums[u]
        return carry

    lax.fori_loop(0, places // UNROLL, rest_step, 0)


def flatten(ref):
    return ref.reshape((ref.shape[0] * ref.shape[1],) + ref.shape[2:])


def first_body(bounds, left_at, right_at, table, ends, got, out):
    out[...] = jnp.zeros(out.shape, out.dtype)
    flat = flatten(got)
    contract(bounds, left_at, right_at, table, ends, flat, flat, out, 0)


def second_body(first, bounds, left_at, right_at, table, ends, got, rest, before, other, mine, acc):
    places = acc.shape[0]
    acc[...] = before[pl.ds(first, places)]
    contract(bounds, left_at, right_at, table, ends, flatten(got), flatten(rest), acc, first)
    other[...] = acc[pl.ds(0, places // 2)]
    mine[...] = acc[pl.ds(places // 2, places // 2)]


def group_table(order, start, stop, slots):
    rows = start.shape[0]
    at = order[:, None] == jnp.arange(rows)[None, :]

    def in_order(values):
        return jnp.sum(jnp.where(at, values[None, :], 0), axis=1)

    start, stop = in_order(start), in_order(stop)
    size = (stop - start) // GROUP
    end = jnp.sum(jnp.where(jnp.arange(rows)[:, None] >= jnp.arange(rows)[None, :], size[None, :], 0), axis=1)
    limit = rows * (slots // GROUP) + 2 * UNROLL
    number = jnp.arange(limit, dtype=jnp.int32)[:, None]
    passed = number >= end[None, :]
    place = jnp.minimum(jnp.sum(passed.astype(jnp.int32), axis=1), rows - 1)
    opened = jnp.max(jnp.where(passed, end[None, :], 0), axis=1)
    mine = place[:, None] == jnp.arange(rows)[None, :]

    def of_place(values):
        return jnp.sum(jnp.where(mine, values[None, :], 0), axis=1)

    base = of_place(start) + (number[:, 0] - opened) * GROUP
    base = jnp.where(number[:, 0] < end[-1], base, slots)
    table = jnp.stack([of_place(order), base, place]).astype(jnp.int32)
    ends = jnp.stack([order, stop, stop - start]).astype(jnp.int32)
    return end.astype(jnp.int32), table, ends


def body(amp_tiles, int_tiles, requests, tri_amp, tri_int, tri_count):
    wanted = requests[0, 0]
    peers, kinds, cap = wanted.shape
    rows, slots = tri_amp.shape[0], tri_amp.shape[2]
    tile = amp_tiles.shape[1:]
    cut = cap // 2
    red = lax.axis_size("red")
    share = rows // red
    steps = red // 2
    me = lax.axis_index("red")

    wanted, me = lax.optimization_barrier((wanted, me))
    asked = lax.all_to_all(wanted.reshape(peers, kinds * cap), "own", split_axis=0, concat_axis=0, tiled=True)
    first_list = tuple((0, s) for s in range(cap)) + tuple((1, s) for s in range(cut))
    second_list = tuple((1, s) for s in range(cut, cap))
    asked, me = lax.optimization_barrier((asked, me))
    send_first, send_second = pack((first_list, second_list), asked, (amp_tiles, int_tiles))
    got_first = lax.all_to_all(send_first, "own", split_axis=0, concat_axis=0, tiled=True)
    got_first, send_second, tri_amp, tri_int, tri_count, me = lax.optimization_barrier(
        (got_first, send_second, tri_amp, tri_int, tri_count, me)
    )
    got_second = lax.all_to_all(send_second, "own", split_axis=0, concat_axis=0, tiled=True)

    amp_pos, int_pos = tri_amp[:, 0], tri_int[:, 0]
    count = tri_count[:, 0]
    alive = lax.broadcasted_iota(jnp.int32, (rows, slots), 1) < count[:, None]
    is_low = int_pos % cap < cut
    key = jnp.where(alive, jnp.where(is_low, 0, 1), 2)
    code = lax.sort((key * peers * cap + amp_pos) * peers * cap + int_pos, dimension=1)
    low = jnp.sum((alive & is_low).astype(jnp.int32), axis=1)
    amp_pos = (code // (peers * cap)) % (peers * cap)
    int_pos = code % (peers * cap)
    pad = ((0, 0), (0, GROUP))
    width = cap + cut
    holder, slot = int_pos // cap, int_pos % cap
    left_at = jnp.pad((amp_pos // cap) * width + amp_pos % cap, pad)
    right_at = jnp.where(slot < cut, holder * width + cap + slot, holder * (cap - cut) + slot - cut)
    right_at = jnp.pad(jnp.where(code < 2 * (peers * cap) ** 2, right_at, 0), pad)

    place = jnp.arange(rows, dtype=jnp.int32)
    step, side = place // (2 * share), (place // share) % 2
    order = (((me // 2 + step) % steps) * 2 + jnp.where(side == 0, 1 - me % 2, me % 2)) * share + place % share
    first_end, first_table, first_ends = group_table(order, jnp.zeros_like(low), low, slots)
    second_end, second_table, second_ends = group_table(order, low, count, slots)
    first_bounds = jnp.pad(first_end[rows - 1 :], (1, 0))
    second_bounds = jnp.pad(second_end[2 * share - 1 :: 2 * share], (1, 0))

    smem = pl.BlockSpec(memory_space=pltpu.SMEM)
    vmem = pl.BlockSpec(memory_space=pltpu.VMEM)
    params = pltpu.CompilerParams(vmem_limit_bytes=24 * 2**20)
    before = pl.pallas_call(
        first_body,
        in_specs=[smem] * 5 + [vmem],
        out_specs=vmem,
        out_shape=jax.ShapeDtypeStruct((rows,) + tile, jnp.float32),
        compiler_params=params,
    )(first_bounds, left_at, right_at, first_table, first_ends, got_first)

    def second(step):
        half = jax.ShapeDtypeStruct((share,) + tile, jnp.float32)
        return pl.pallas_call(
            functools.partial(second_body, step * 2 * share),
            in_specs=[smem] * 5 + [vmem] * 3,
            out_specs=[vmem, vmem],
            out_shape=[half, half],
            scratch_shapes=[pltpu.VMEM((2 * share,) + tile, jnp.float32)],
            compiler_params=params,
        )(second_bounds, left_at, right_at, second_table, second_ends, got_first, got_second, before)

    swap = [(i, i ^ 1) for i in range(red)]

    def met(step):
        other, mine = second(step)
        return mine + lax.ppermute(other, "red", swap)

    arrived = []
    for step in far_first(steps)[:-1]:
        block = met(step)
        arrived.append(lax.ppermute(block, "red", [(i, ((i // 2 + step) % steps) * 2 + i % 2) for i in range(red)]))
    total = met(0)
    for block in arrived:
        total = total + block
    return total


def far_first(steps):
    return [steps // 2] + [s for s in range(1, steps) if s != steps // 2] + [0]


def solution(mesh):
    placed = (
        P(("own", "red"), None, None),
        P(("own", "red"), None, None),
        P("own", "red", None, None, None),
        P("own", "red", None),
        P("own", "red", None),
        P("own", "red"),
    )

    return jax.shard_map(body, mesh=mesh, in_specs=placed, out_specs=P(("own", "red"), None, None), check_vma=False)
```

```python
import functools

import jax
import jax.numpy as jnp
from jax import lax
from jax.experimental import pallas as pl
from jax.experimental.pallas import tpu as pltpu
from jax.sharding import PartitionSpec as P

GROUP = 4
UNROLL = 4
PACK_STEPS = 4


def pack_body(lists, asked, *refs):
    stores, outs = refs[:2], refs[2:]
    cap = asked.shape[1] // 2
    last = stores[0].shape[0] - 1
    peers = outs[0].shape[0]
    first = pl.program_id(0) * peers
    for peer in range(peers):
        for out, picks in zip(outs, lists):
            for pos, (kind, slot) in enumerate(picks):
                tile = jnp.clip(asked[first + peer, kind * cap + slot], 0, last)
                out[peer, pos] = stores[kind][tile]


def pack(lists, asked, stores):
    peers = asked.shape[0]
    tile = stores[0].shape[1:]
    whole = pl.BlockSpec(stores[0].shape, lambda i: (0, 0, 0))
    return pl.pallas_call(
        functools.partial(pack_body, lists),
        grid=(PACK_STEPS,),
        in_specs=[pl.BlockSpec(memory_space=pltpu.SMEM), whole, whole],
        out_specs=[
            pl.BlockSpec((peers // PACK_STEPS, len(picks)) + tile, lambda i: (i, 0, 0, 0)) for picks in lists
        ],
        out_shape=[jax.ShapeDtypeStruct((peers, len(picks)) + tile, stores[0].dtype) for picks in lists],
    )(asked, *stores)


def group_dot(lefts, rights):
    return lax.dot_general(
        jnp.concatenate(lefts, axis=1),
        jnp.concatenate(rights, axis=1),
        (((1,), (1,)), ((), ())),
        preferred_element_type=jnp.float32,
    )


def contract(bounds, left_at, right_at, table, ends, left, right, acc, first):
    places = acc.shape[0]
    begin, finish = bounds[first // places], bounds[first // places + 1]

    def full_step(i, carry):
        sums = []
        for u in range(UNROLL):
            g = begin + i * UNROLL + u
            row, base = table[0, g], table[1, g]
            lefts = [left[left_at[row, base + j]] for j in range(GROUP)]
            rights = [right[right_at[row, base + j]] for j in range(GROUP)]
            sums.append(group_dot(lefts, rights))
        for u in range(UNROLL):
            g = begin + i * UNROLL + u
            place = jnp.minimum(table[2, g] - first, places - 1)
            acc[place] = acc[place] + jnp.where(g < finish, sums[u], 0.0)
        return carry

    lax.fori_loop(0, (finish - begin + UNROLL - 1) // UNROLL, full_step, 0)

    def rest_step(i, carry):
        sums = []
        for u in range(UNROLL):
            place = first + i * UNROLL + u
            row, stop = ends[0, place], ends[1, place]
            base = stop - ends[2, place] % GROUP
            lefts, rights = [], []
            for j in range(GROUP):
                tile = left[left_at[row, base + j]]
                lefts.append(jnp.where(base + j < stop, tile, jnp.zeros_like(tile)))
                rights.append(right[right_at[row, base + j]])
            sums.append(group_dot(lefts, rights))
        for u in range(UNROLL):
            place = i * UNROLL + u
            acc[place] = acc[place] + sums[u]
        return carry

    lax.fori_loop(0, places // UNROLL, rest_step, 0)


def flatten(ref):
    return ref.reshape((ref.shape[0] * ref.shape[1],) + ref.shape[2:])


def first_body(bounds, left_at, right_at, table, ends, got, out):
    out[...] = jnp.zeros(out.shape, out.dtype)
    flat = flatten(got)
    contract(bounds, left_at, right_at, table, ends, flat, flat, out, 0)


def second_body(first, bounds, left_at, right_at, table, ends, got, rest, before, other, mine, acc, old, sem):
    places = acc.shape[0]
    copy = pltpu.make_async_copy(before.at[pl.ds(first, places)], old, sem)
    copy.start()
    acc[...] = jnp.zeros(acc.shape, acc.dtype)
    contract(bounds, left_at, right_at, table, ends, flatten(got), flatten(rest), acc, first)
    copy.wait()
    for half, out in enumerate((other, mine)):
        span = pl.ds(half * (places // 2), places // 2)
        out[...] = acc[span] + old[span]


def group_table(order, start, stop, slots):
    rows = start.shape[0]
    at = order[:, None] == jnp.arange(rows)[None, :]

    def in_order(values):
        return jnp.sum(jnp.where(at, values[None, :], 0), axis=1)

    start, stop = in_order(start), in_order(stop)
    size = (stop - start) // GROUP
    end = jnp.sum(jnp.where(jnp.arange(rows)[:, None] >= jnp.arange(rows)[None, :], size[None, :], 0), axis=1)
    limit = rows * (slots // GROUP) + 2 * UNROLL
    number = jnp.arange(limit, dtype=jnp.int32)[:, None]
    passed = number >= end[None, :]
    place = jnp.minimum(jnp.sum(passed.astype(jnp.int32), axis=1), rows - 1)
    opened = jnp.max(jnp.where(passed, end[None, :], 0), axis=1)
    mine = place[:, None] == jnp.arange(rows)[None, :]

    def of_place(values):
        return jnp.sum(jnp.where(mine, values[None, :], 0), axis=1)

    base = of_place(start) + (number[:, 0] - opened) * GROUP
    base = jnp.where(number[:, 0] < end[-1], base, slots)
    table = jnp.stack([of_place(order), base, place]).astype(jnp.int32)
    ends = jnp.stack([order, stop, stop - start]).astype(jnp.int32)
    return end.astype(jnp.int32), table, ends


def body(amp_tiles, int_tiles, requests, tri_amp, tri_int, tri_count):
    wanted = requests[0, 0]
    peers, kinds, cap = wanted.shape
    rows, slots = tri_amp.shape[0], tri_amp.shape[2]
    tile = amp_tiles.shape[1:]
    cut = cap // 2
    red = lax.axis_size("red")
    share = rows // red
    steps = red // 2
    me = lax.axis_index("red")

    wanted, me = lax.optimization_barrier((wanted, me))
    asked = lax.all_to_all(wanted.reshape(peers, kinds * cap), "own", split_axis=0, concat_axis=0, tiled=True)
    first_list = tuple((0, s) for s in range(cap)) + tuple((1, s) for s in range(cut))
    second_list = tuple((1, s) for s in range(cut, cap))
    asked, me = lax.optimization_barrier((asked, me))
    send_first, send_second = pack((first_list, second_list), asked, (amp_tiles, int_tiles))
    got_first = lax.all_to_all(send_first, "own", split_axis=0, concat_axis=0, tiled=True)
    got_first, send_second, tri_amp, tri_int, tri_count, me = lax.optimization_barrier(
        (got_first, send_second, tri_amp, tri_int, tri_count, me)
    )
    got_second = lax.all_to_all(send_second, "own", split_axis=0, concat_axis=0, tiled=True)

    amp_pos, int_pos = tri_amp[:, 0], tri_int[:, 0]
    count = tri_count[:, 0]
    alive = lax.broadcasted_iota(jnp.int32, (rows, slots), 1) < count[:, None]
    is_low = int_pos % cap < cut
    key = jnp.where(alive, jnp.where(is_low, 0, 1), 2)
    code = lax.sort((key * peers * cap + amp_pos) * peers * cap + int_pos, dimension=1)
    low = jnp.sum((alive & is_low).astype(jnp.int32), axis=1)
    amp_pos = (code // (peers * cap)) % (peers * cap)
    int_pos = code % (peers * cap)
    pad = ((0, 0), (0, GROUP))
    width = cap + cut
    holder, slot = int_pos // cap, int_pos % cap
    left_at = jnp.pad((amp_pos // cap) * width + amp_pos % cap, pad)
    right_at = jnp.where(slot < cut, holder * width + cap + slot, holder * (cap - cut) + slot - cut)
    right_at = jnp.pad(jnp.where(code < 2 * (peers * cap) ** 2, right_at, 0), pad)

    place = jnp.arange(rows, dtype=jnp.int32)
    step, side = place // (2 * share), (place // share) % 2
    order = (((me // 2 + step) % steps) * 2 + jnp.where(side == 0, 1 - me % 2, me % 2)) * share + place % share
    first_end, first_table, first_ends = group_table(order, jnp.zeros_like(low), low, slots)
    second_end, second_table, second_ends = group_table(order, low, count, slots)
    first_bounds = jnp.pad(first_end[rows - 1 :], (1, 0))
    second_bounds = jnp.pad(second_end[2 * share - 1 :: 2 * share], (1, 0))

    smem = pl.BlockSpec(memory_space=pltpu.SMEM)
    vmem = pl.BlockSpec(memory_space=pltpu.VMEM)
    params = pltpu.CompilerParams(vmem_limit_bytes=24 * 2**20)
    before = pl.pallas_call(
        first_body,
        in_specs=[smem] * 5 + [vmem],
        out_specs=vmem,
        out_shape=jax.ShapeDtypeStruct((rows,) + tile, jnp.float32),
        compiler_params=params,
    )(first_bounds, left_at, right_at, first_table, first_ends, got_first)

    before = pltpu.with_memory_space_constraint(before, pltpu.HBM)

    def second(step):
        half = jax.ShapeDtypeStruct((share,) + tile, jnp.float32)
        return pl.pallas_call(
            functools.partial(second_body, step * 2 * share),
            in_specs=[smem] * 5 + [vmem] * 2 + [pl.BlockSpec(memory_space=pltpu.HBM)],
            out_specs=[vmem, vmem],
            out_shape=[half, half],
            scratch_shapes=[pltpu.VMEM((2 * share,) + tile, jnp.float32)] * 2 + [pltpu.SemaphoreType.DMA(())],
            compiler_params=params,
        )(second_bounds, left_at, right_at, second_table, second_ends, got_first, got_second, before)

    swap = [(i, i ^ 1) for i in range(red)]

    def met(step, spans=(slice(None),), extra=0.0):
        other, mine = second(step)
        theirs = lax.ppermute(other, "red", swap)
        return [mine[span] + theirs[span] + extra for span in spans]

    def send(value, distance):
        return lax.ppermute(value, "red", [(i, ((i // 2 + distance) % steps) * 2 + i % 2) for i in range(red)])

    half = share // 2
    far_low, far_high = met(2, (slice(0, half), slice(half, share)))
    from_left = send(far_low, 1)
    from_right = send(far_high, -1)
    still = ((0, 0), (0, 0))
    (right,) = met(1, extra=jnp.pad(from_left, ((0, share - half), *still)))
    from_left = send(right, 1)
    (left,) = met(3, extra=jnp.pad(from_right, ((half, 0), *still)))
    from_right = send(left, -1)
    return met(0)[0] + from_left + from_right


def solution(mesh):
    placed = (
        P(("own", "red"), None, None),
        P(("own", "red"), None, None),
        P("own", "red", None, None, None),
        P("own", "red", None),
        P("own", "red", None),
        P("own", "red"),
    )

    return jax.shard_map(body, mesh=mesh, in_specs=placed, out_specs=P(("own", "red"), None, None), check_vma=False)
```

```python
import functools

import jax
import jax.numpy as jnp
from jax import lax
from jax.experimental import pallas as pl
from jax.experimental.pallas import tpu as pltpu
from jax.sharding import PartitionSpec as P

GROUP = 4
UNROLL = 4
PACK_STEPS = 4


def pack_body(lists, asked, *refs):
    stores, outs = refs[:2], refs[2:]
    cap = asked.shape[1] // 2
    last = stores[0].shape[0] - 1
    peers = outs[0].shape[0]
    first = pl.program_id(0) * peers
    for peer in range(peers):
        for out, picks in zip(outs, lists):
            for pos, (kind, slot) in enumerate(picks):
                tile = jnp.clip(asked[first + peer, kind * cap + slot], 0, last)
                out[peer, pos] = stores[kind][tile]


def pack(lists, asked, stores):
    peers = asked.shape[0]
    tile = stores[0].shape[1:]
    whole = pl.BlockSpec(stores[0].shape, lambda i: (0, 0, 0))
    return pl.pallas_call(
        functools.partial(pack_body, lists),
        grid=(PACK_STEPS,),
        in_specs=[pl.BlockSpec(memory_space=pltpu.SMEM), whole, whole],
        out_specs=[
            pl.BlockSpec((peers // PACK_STEPS, len(picks)) + tile, lambda i: (i, 0, 0, 0)) for picks in lists
        ],
        out_shape=[jax.ShapeDtypeStruct((peers, len(picks)) + tile, stores[0].dtype) for picks in lists],
    )(asked, *stores)


def group_dot(lefts, rights):
    return lax.dot_general(
        jnp.concatenate(lefts, axis=1),
        jnp.concatenate(rights, axis=1),
        (((1,), (1,)), ((), ())),
        preferred_element_type=jnp.float32,
    )


def contract(bounds, left_at, right_at, table, ends, left, right, acc, first):
    places = acc.shape[0]
    begin, finish = bounds[first // places], bounds[first // places + 1]

    def full_step(i, carry):
        sums = []
        for u in range(UNROLL):
            g = begin + i * UNROLL + u
            row, base = table[0, g], table[1, g]
            lefts = [left[left_at[row, base + j]] for j in range(GROUP)]
            rights = [right[right_at[row, base + j]] for j in range(GROUP)]
            sums.append(group_dot(lefts, rights))
        for u in range(UNROLL):
            g = begin + i * UNROLL + u
            place = jnp.minimum(table[2, g] - first, places - 1)
            acc[place] = acc[place] + jnp.where(g < finish, sums[u], 0.0)
        return carry

    lax.fori_loop(0, (finish - begin + UNROLL - 1) // UNROLL, full_step, 0)

    def rest_step(i, carry):
        sums = []
        for u in range(UNROLL):
            place = first + i * UNROLL + u
            row, stop = ends[0, place], ends[1, place]
            base = stop - ends[2, place] % GROUP
            lefts, rights = [], []
            for j in range(GROUP):
                tile = left[left_at[row, base + j]]
                lefts.append(jnp.where(base + j < stop, tile, jnp.zeros_like(tile)))
                rights.append(right[right_at[row, base + j]])
            sums.append(group_dot(lefts, rights))
        for u in range(UNROLL):
            place = i * UNROLL + u
            acc[place] = acc[place] + sums[u]
        return carry

    lax.fori_loop(0, places // UNROLL, rest_step, 0)


def flatten(ref):
    return ref.reshape((ref.shape[0] * ref.shape[1],) + ref.shape[2:])


def first_body(bounds, left_at, right_at, table, ends, got, out, acc, sem):
    acc[...] = jnp.zeros(acc.shape, acc.dtype)
    flat = flatten(got)
    contract(bounds, left_at, right_at, table, ends, flat, flat, acc, 0)
    copy = pltpu.make_async_copy(acc, out, sem)
    copy.start()
    copy.wait()


def second_body(first, bounds, left_at, right_at, table, ends, got, rest, before, other, mine, acc, old, sem):
    places = acc.shape[0]
    copy = pltpu.make_async_copy(before.at[pl.ds(first, places)], old, sem)
    copy.start()
    acc[...] = jnp.zeros(acc.shape, acc.dtype)
    contract(bounds, left_at, right_at, table, ends, flatten(got), flatten(rest), acc, first)
    copy.wait()
    for half, out in enumerate((other, mine)):
        span = pl.ds(half * (places // 2), places // 2)
        out[...] = acc[span] + old[span]


def group_table(order, start, stop, slots):
    rows = start.shape[0]
    at = order[:, None] == jnp.arange(rows)[None, :]

    def in_order(values):
        return jnp.sum(jnp.where(at, values[None, :], 0), axis=1)

    start, stop = in_order(start), in_order(stop)
    size = (stop - start) // GROUP
    end = jnp.sum(jnp.where(jnp.arange(rows)[:, None] >= jnp.arange(rows)[None, :], size[None, :], 0), axis=1)
    limit = rows * (slots // GROUP) + 2 * UNROLL
    number = jnp.arange(limit, dtype=jnp.int32)[:, None]
    passed = number >= end[None, :]
    place = jnp.minimum(jnp.sum(passed.astype(jnp.int32), axis=1), rows - 1)
    opened = jnp.max(jnp.where(passed, end[None, :], 0), axis=1)
    mine = place[:, None] == jnp.arange(rows)[None, :]

    def of_place(values):
        return jnp.sum(jnp.where(mine, values[None, :], 0), axis=1)

    base = of_place(start) + (number[:, 0] - opened) * GROUP
    base = jnp.where(number[:, 0] < end[-1], base, slots)
    table = jnp.stack([of_place(order), base, place]).astype(jnp.int32)
    ends = jnp.stack([order, stop, stop - start]).astype(jnp.int32)
    return end.astype(jnp.int32), table, ends


def body(amp_tiles, int_tiles, requests, tri_amp, tri_int, tri_count):
    wanted = requests[0, 0]
    peers, kinds, cap = wanted.shape
    rows, slots = tri_amp.shape[0], tri_amp.shape[2]
    tile = amp_tiles.shape[1:]
    cut = cap - 3
    red = lax.axis_size("red")
    share = rows // red
    steps = red // 2
    me = lax.axis_index("red")

    asked = lax.all_to_all(wanted.reshape(peers, kinds * cap), "own", split_axis=0, concat_axis=0, tiled=True)
    amp_pos, int_pos = tri_amp[:, 0], tri_int[:, 0]
    count = tri_count[:, 0]
    alive = lax.broadcasted_iota(jnp.int32, (rows, slots), 1) < count[:, None]
    is_low = int_pos % cap < cut
    key = jnp.where(alive, jnp.where(is_low, 0, 1), 2)
    code = lax.sort((key * peers * cap + amp_pos) * peers * cap + int_pos, dimension=1)
    low = jnp.sum((alive & is_low).astype(jnp.int32), axis=1)
    amp_pos = (code // (peers * cap)) % (peers * cap)
    int_pos = code % (peers * cap)
    pad = ((0, 0), (0, GROUP))
    width = cap + cut
    holder, slot = int_pos // cap, int_pos % cap
    left_at = jnp.pad((amp_pos // cap) * width + amp_pos % cap, pad)
    right_at = jnp.where(slot < cut, holder * width + cap + slot, holder * (cap - cut) + slot - cut)
    right_at = jnp.pad(jnp.where(code < 2 * (peers * cap) ** 2, right_at, 0), pad)

    place = jnp.arange(rows, dtype=jnp.int32)
    step, side = place // (2 * share), (place // share) % 2
    order = (((me // 2 + step) % steps) * 2 + jnp.where(side == 0, 1 - me % 2, me % 2)) * share + place % share
    first_end, first_table, first_ends = group_table(order, jnp.zeros_like(low), low, slots)
    second_end, second_table, second_ends = group_table(order, low, count, slots)
    first_bounds = jnp.pad(first_end[rows - 1 :], (1, 0))
    second_bounds = jnp.pad(second_end[2 * share - 1 :: 2 * share], (1, 0))

    tables = (left_at, right_at, first_bounds, first_table, first_ends, second_bounds, second_table, second_ends)
    asked, tables = lax.optimization_barrier((asked, tables))
    first_list = tuple((0, s) for s in range(cap)) + tuple((1, s) for s in range(cut))
    second_list = tuple((1, s) for s in range(cut, cap))
    send_first, send_second = pack((first_list, second_list), asked, (amp_tiles, int_tiles))
    got_first = lax.all_to_all(send_first, "own", split_axis=0, concat_axis=0, tiled=True)
    got_first, send_second, tables = lax.optimization_barrier((got_first, send_second, tables))
    left_at, right_at, first_bounds, first_table, first_ends, second_bounds, second_table, second_ends = tables
    got_second = lax.all_to_all(send_second, "own", split_axis=0, concat_axis=0, tiled=True)

    smem = pl.BlockSpec(memory_space=pltpu.SMEM)
    vmem = pl.BlockSpec(memory_space=pltpu.VMEM)
    params = pltpu.CompilerParams(vmem_limit_bytes=24 * 2**20)
    before = pl.pallas_call(
        first_body,
        in_specs=[smem] * 5 + [vmem],
        out_specs=pl.BlockSpec(memory_space=pltpu.HBM),
        out_shape=pltpu.HBM((rows,) + tile, jnp.float32),
        scratch_shapes=[pltpu.VMEM((rows,) + tile, jnp.float32), pltpu.SemaphoreType.DMA(())],
        compiler_params=params,
    )(first_bounds, left_at, right_at, first_table, first_ends, got_first)

    before = pltpu.with_memory_space_constraint(before, pltpu.HBM)

    def second(step):
        half = jax.ShapeDtypeStruct((share,) + tile, jnp.float32)
        return pl.pallas_call(
            functools.partial(second_body, step * 2 * share),
            in_specs=[smem] * 5 + [vmem] * 2 + [pl.BlockSpec(memory_space=pltpu.HBM)],
            out_specs=[vmem, vmem],
            out_shape=[half, half],
            scratch_shapes=[pltpu.VMEM((2 * share,) + tile, jnp.float32)] * 2 + [pltpu.SemaphoreType.DMA(())],
            compiler_params=params,
        )(second_bounds, left_at, right_at, second_table, second_ends, got_first, got_second, before)

    swap = [(i, i ^ 1) for i in range(red)]

    def met(step, spans=(slice(None),), extra=0.0):
        other, mine = second(step)
        theirs = lax.ppermute(other, "red", swap)
        return [mine[span] + theirs[span] + extra for span in spans]

    def send(value, distance):
        return lax.ppermute(value, "red", [(i, ((i // 2 + distance) % steps) * 2 + i % 2) for i in range(red)])

    half = share // 2
    far_low, far_high = met(2, (slice(0, half), slice(half, share)))
    from_left = send(far_low, 1)
    from_right = send(far_high, -1)
    still = ((0, 0), (0, 0))
    (right,) = met(1, extra=jnp.pad(from_left, ((0, share - half), *still)))
    from_left = send(right, 1)
    (left,) = met(3, extra=jnp.pad(from_right, ((half, 0), *still)))
    from_right = send(left, -1)
    return met(0)[0] + from_left + from_right


def solution(mesh):
    placed = (
        P(("own", "red"), None, None),
        P(("own", "red"), None, None),
        P("own", "red", None, None, None),
        P("own", "red", None),
        P("own", "red", None),
        P("own", "red"),
    )

    return jax.shard_map(body, mesh=mesh, in_specs=placed, out_specs=P(("own", "red"), None, None), check_vma=False)
```

```python
import functools

import jax
import jax.numpy as jnp
from jax import lax
from jax.experimental import pallas as pl
from jax.experimental.pallas import tpu as pltpu
from jax.sharding import PartitionSpec as P

GROUP = 8
UNROLL = 4
PACK_STEPS = 4


def pack_body(lists, asked, *refs):
    stores, outs = refs[:2], refs[2:]
    cap = asked.shape[1] // 2
    last = stores[0].shape[0] - 1
    peers = outs[0].shape[0]
    first = pl.program_id(0) * peers
    for peer in range(peers):
        for out, picks in zip(outs, lists):
            for pos, (kind, slot) in enumerate(picks):
                tile = jnp.clip(asked[first + peer, kind * cap + slot], 0, last)
                out[peer, pos] = stores[kind][tile]


def pack(lists, asked, stores):
    peers = asked.shape[0]
    tile = stores[0].shape[1:]
    whole = pl.BlockSpec(stores[0].shape, lambda i: (0, 0, 0))
    return pl.pallas_call(
        functools.partial(pack_body, lists),
        grid=(PACK_STEPS,),
        in_specs=[pl.BlockSpec(memory_space=pltpu.SMEM), whole, whole],
        out_specs=[
            pl.BlockSpec((peers // PACK_STEPS, len(picks)) + tile, lambda i: (i, 0, 0, 0)) for picks in lists
        ],
        out_shape=[jax.ShapeDtypeStruct((peers, len(picks)) + tile, stores[0].dtype) for picks in lists],
    )(asked, *stores)


def group_dot(lefts, rights):
    return lax.dot_general(
        jnp.concatenate(lefts, axis=1),
        jnp.concatenate(rights, axis=1),
        (((1,), (1,)), ((), ())),
        preferred_element_type=jnp.float32,
    )


def contract(bounds, left_at, right_at, table, ends, left, right, acc, first):
    places = acc.shape[0]
    begin, finish = bounds[first // places], bounds[first // places + 1]

    def full_step(i, carry):
        sums = []
        for u in range(UNROLL):
            g = begin + i * UNROLL + u
            row, base = table[0, g], table[1, g]
            lefts = [left[left_at[row, base + j]] for j in range(GROUP)]
            rights = [right[right_at[row, base + j]] for j in range(GROUP)]
            sums.append(group_dot(lefts, rights))
        for u in range(UNROLL):
            g = begin + i * UNROLL + u
            place = jnp.minimum(table[2, g] - first, places - 1)
            acc[place] = acc[place] + jnp.where(g < finish, sums[u], 0.0)
        return carry

    lax.fori_loop(0, (finish - begin + UNROLL - 1) // UNROLL, full_step, 0)

    def rest_step(i, carry):
        sums = []
        for u in range(UNROLL):
            place = first + i * UNROLL + u
            row, stop = ends[0, place], ends[1, place]
            base = stop - ends[2, place] % GROUP
            lefts, rights = [], []
            for j in range(GROUP):
                tile = left[left_at[row, base + j]]
                lefts.append(jnp.where(base + j < stop, tile, jnp.zeros_like(tile)))
                rights.append(right[right_at[row, base + j]])
            sums.append(group_dot(lefts, rights))
        for u in range(UNROLL):
            place = i * UNROLL + u
            acc[place] = acc[place] + sums[u]
        return carry

    lax.fori_loop(0, places // UNROLL, rest_step, 0)


def flatten(ref):
    return ref.reshape((ref.shape[0] * ref.shape[1],) + ref.shape[2:])


def first_body(bounds, left_at, right_at, table, ends, got, out, acc, sem):
    acc[...] = jnp.zeros(acc.shape, acc.dtype)
    flat = flatten(got)
    contract(bounds, left_at, right_at, table, ends, flat, flat, acc, 0)
    copy = pltpu.make_async_copy(acc, out, sem)
    copy.start()
    copy.wait()


def second_body(first, bounds, left_at, right_at, table, ends, got, rest, before, other, mine, acc, old, sem):
    places = acc.shape[0]
    copy = pltpu.make_async_copy(before.at[pl.ds(first, places)], old, sem)
    copy.start()
    acc[...] = jnp.zeros(acc.shape, acc.dtype)
    contract(bounds, left_at, right_at, table, ends, flatten(got), flatten(rest), acc, first)
    copy.wait()
    for half, out in enumerate((other, mine)):
        span = pl.ds(half * (places // 2), places // 2)
        out[...] = acc[span] + old[span]


def group_table(order, start, stop, slots):
    rows = start.shape[0]
    at = order[:, None] == jnp.arange(rows)[None, :]

    def in_order(values):
        return jnp.sum(jnp.where(at, values[None, :], 0), axis=1)

    start, stop = in_order(start), in_order(stop)
    size = (stop - start) // GROUP
    end = jnp.sum(jnp.where(jnp.arange(rows)[:, None] >= jnp.arange(rows)[None, :], size[None, :], 0), axis=1)
    limit = rows * (slots // GROUP) + 2 * UNROLL
    number = jnp.arange(limit, dtype=jnp.int32)[:, None]
    passed = number >= end[None, :]
    place = jnp.minimum(jnp.sum(passed.astype(jnp.int32), axis=1), rows - 1)
    opened = jnp.max(jnp.where(passed, end[None, :], 0), axis=1)
    mine = place[:, None] == jnp.arange(rows)[None, :]

    def of_place(values):
        return jnp.sum(jnp.where(mine, values[None, :], 0), axis=1)

    base = of_place(start) + (number[:, 0] - opened) * GROUP
    base = jnp.where(number[:, 0] < end[-1], base, slots)
    table = jnp.stack([of_place(order), base, place]).astype(jnp.int32)
    ends = jnp.stack([order, stop, stop - start]).astype(jnp.int32)
    return end.astype(jnp.int32), table, ends


def body(amp_tiles, int_tiles, requests, tri_amp, tri_int, tri_count):
    wanted = requests[0, 0]
    peers, kinds, cap = wanted.shape
    rows, slots = tri_amp.shape[0], tri_amp.shape[2]
    tile = amp_tiles.shape[1:]
    cut = cap // 2
    red = lax.axis_size("red")
    share = rows // red
    steps = red // 2
    me = lax.axis_index("red")

    wanted, me = lax.optimization_barrier((wanted, me))
    asked = lax.all_to_all(wanted.reshape(peers, kinds * cap), "own", split_axis=0, concat_axis=0, tiled=True)
    first_list = tuple((0, s) for s in range(cap)) + tuple((1, s) for s in range(cut))
    second_list = tuple((1, s) for s in range(cut, cap))
    asked, me = lax.optimization_barrier((asked, me))
    send_first, send_second = pack((first_list, second_list), asked, (amp_tiles, int_tiles))
    got_first = lax.all_to_all(send_first, "own", split_axis=0, concat_axis=0, tiled=True)
    got_first, send_second, tri_amp, tri_int, tri_count, me = lax.optimization_barrier(
        (got_first, send_second, tri_amp, tri_int, tri_count, me)
    )
    got_second = lax.all_to_all(send_second, "own", split_axis=0, concat_axis=0, tiled=True)

    amp_pos, int_pos = tri_amp[:, 0], tri_int[:, 0]
    count = tri_count[:, 0]
    alive = lax.broadcasted_iota(jnp.int32, (rows, slots), 1) < count[:, None]
    is_low = int_pos % cap < cut
    key = jnp.where(alive, jnp.where(is_low, 0, 1), 2)
    code = lax.sort((key * peers * cap + amp_pos) * peers * cap + int_pos, dimension=1)
    low = jnp.sum((alive & is_low).astype(jnp.int32), axis=1)
    amp_pos = (code // (peers * cap)) % (peers * cap)
    int_pos = code % (peers * cap)
    pad = ((0, 0), (0, GROUP))
    width = cap + cut
    holder, slot = int_pos // cap, int_pos % cap
    left_at = jnp.pad((amp_pos // cap) * width + amp_pos % cap, pad)
    right_at = jnp.where(slot < cut, holder * width + cap + slot, holder * (cap - cut) + slot - cut)
    right_at = jnp.pad(jnp.where(code < 2 * (peers * cap) ** 2, right_at, 0), pad)

    place = jnp.arange(rows, dtype=jnp.int32)
    step, side = place // (2 * share), (place // share) % 2
    order = (((me // 2 + step) % steps) * 2 + jnp.where(side == 0, 1 - me % 2, me % 2)) * share + place % share
    first_end, first_table, first_ends = group_table(order, jnp.zeros_like(low), low, slots)
    second_end, second_table, second_ends = group_table(order, low, count, slots)
    first_bounds = jnp.pad(first_end[rows - 1 :], (1, 0))
    second_bounds = jnp.pad(second_end[2 * share - 1 :: 2 * share], (1, 0))

    smem = pl.BlockSpec(memory_space=pltpu.SMEM)
    vmem = pl.BlockSpec(memory_space=pltpu.VMEM)
    params = pltpu.CompilerParams(vmem_limit_bytes=24 * 2**20)
    before = pl.pallas_call(
        first_body,
        in_specs=[smem] * 5 + [vmem],
        out_specs=pl.BlockSpec(memory_space=pltpu.HBM),
        out_shape=pltpu.HBM((rows,) + tile, jnp.float32),
        scratch_shapes=[pltpu.VMEM((rows,) + tile, jnp.float32), pltpu.SemaphoreType.DMA(())],
        compiler_params=params,
    )(first_bounds, left_at, right_at, first_table, first_ends, got_first)

    before = pltpu.with_memory_space_constraint(before, pltpu.HBM)

    def second(step):
        half = jax.ShapeDtypeStruct((share,) + tile, jnp.float32)
        return pl.pallas_call(
            functools.partial(second_body, step * 2 * share),
            in_specs=[smem] * 5 + [vmem] * 2 + [pl.BlockSpec(memory_space=pltpu.HBM)],
            out_specs=[vmem, vmem],
            out_shape=[half, half],
            scratch_shapes=[pltpu.VMEM((2 * share,) + tile, jnp.float32)] * 2 + [pltpu.SemaphoreType.DMA(())],
            compiler_params=params,
        )(second_bounds, left_at, right_at, second_table, second_ends, got_first, got_second, before)

    swap = [(i, i ^ 1) for i in range(red)]

    def met(step, spans=(slice(None),), extra=0.0):
        other, mine = second(step)
        theirs = lax.ppermute(other, "red", swap)
        return [mine[span] + theirs[span] + extra for span in spans]

    def send(value, distance):
        return lax.ppermute(value, "red", [(i, ((i // 2 + distance) % steps) * 2 + i % 2) for i in range(red)])

    half = share // 2
    far_low, far_high = met(2, (slice(0, half), slice(half, share)))
    from_left = send(far_low, 1)
    from_right = send(far_high, -1)
    still = ((0, 0), (0, 0))
    (right,) = met(1, extra=jnp.pad(from_left, ((0, share - half), *still)))
    from_left = send(right, 1)
    (left,) = met(3, extra=jnp.pad(from_right, ((half, 0), *still)))
    from_right = send(left, -1)
    return met(0)[0] + from_left + from_right


def solution(mesh):
    placed = (
        P(("own", "red"), None, None),
        P(("own", "red"), None, None),
        P("own", "red", None, None, None),
        P("own", "red", None),
        P("own", "red", None),
        P("own", "red"),
    )

    return jax.shard_map(body, mesh=mesh, in_specs=placed, out_specs=P(("own", "red"), None, None), check_vma=False)
```

```python
import functools

import jax
import jax.numpy as jnp
from jax import lax
from jax.experimental import pallas as pl
from jax.experimental.pallas import tpu as pltpu
from jax.sharding import PartitionSpec as P

GROUP = 8
UNROLL = 4
PACK_STEPS = 8


def pack_body(lists, asked, *refs):
    stores, outs = refs[:2], refs[2:]
    cap = asked.shape[1] // 2
    last = stores[0].shape[0] - 1
    peers = outs[0].shape[0]
    first = pl.program_id(0) * peers
    for peer in range(peers):
        for out, picks in zip(outs, lists):
            for pos, (kind, slot) in enumerate(picks):
                tile = jnp.clip(asked[first + peer, kind * cap + slot], 0, last)
                out[peer, pos] = stores[kind][tile]


def pack(lists, asked, stores):
    peers = asked.shape[0]
    tile = stores[0].shape[1:]
    whole = pl.BlockSpec(memory_space=pltpu.VMEM)
    return pl.pallas_call(
        functools.partial(pack_body, lists),
        grid=(PACK_STEPS,),
        in_specs=[pl.BlockSpec(memory_space=pltpu.SMEM), whole, whole],
        out_specs=[
            pl.BlockSpec((peers // PACK_STEPS, len(picks)) + tile, lambda i: (i, 0, 0, 0)) for picks in lists
        ],
        out_shape=[jax.ShapeDtypeStruct((peers, len(picks)) + tile, stores[0].dtype) for picks in lists],
        compiler_params=pltpu.CompilerParams(vmem_limit_bytes=24 * 2**20),
    )(asked, *stores)


def group_dot(lefts, rights):
    return lax.dot_general(
        jnp.concatenate(lefts, axis=1),
        jnp.concatenate(rights, axis=1),
        (((1,), (1,)), ((), ())),
        preferred_element_type=jnp.float32,
    )


def contract(bounds, left_at, right_at, table, ends, left, right, acc, first):
    places = acc.shape[0]
    begin, finish = bounds[first // places], bounds[first // places + 1]

    def full_step(i, carry):
        sums = []
        for u in range(UNROLL):
            g = begin + i * UNROLL + u
            row, base = table[0, g], table[1, g]
            lefts = [left[left_at[row, base + j]] for j in range(GROUP)]
            rights = [right[right_at[row, base + j]] for j in range(GROUP)]
            sums.append(group_dot(lefts, rights))
        for u in range(UNROLL):
            g = begin + i * UNROLL + u
            place = jnp.minimum(table[2, g] - first, places - 1)
            acc[place] = acc[place] + jnp.where(g < finish, sums[u], 0.0)
        return carry

    lax.fori_loop(0, (finish - begin + UNROLL - 1) // UNROLL, full_step, 0)

    def rest_step(i, carry):
        sums = []
        for u in range(UNROLL):
            place = first + i * UNROLL + u
            row, stop = ends[0, place], ends[1, place]
            base = stop - ends[2, place] % GROUP
            lefts, rights = [], []
            for j in range(GROUP):
                tile = left[left_at[row, base + j]]
                lefts.append(jnp.where(base + j < stop, tile, jnp.zeros_like(tile)))
                rights.append(right[right_at[row, base + j]])
            sums.append(group_dot(lefts, rights))
        for u in range(UNROLL):
            place = i * UNROLL + u
            acc[place] = acc[place] + sums[u]
        return carry

    lax.fori_loop(0, places // UNROLL, rest_step, 0)


def flatten(ref):
    return ref.reshape((ref.shape[0] * ref.shape[1],) + ref.shape[2:])


def first_body(bounds, left_at, right_at, table, ends, got, out, acc, sem):
    acc[...] = jnp.zeros(acc.shape, acc.dtype)
    flat = flatten(got)
    contract(bounds, left_at, right_at, table, ends, flat, flat, acc, 0)
    copy = pltpu.make_async_copy(acc, out, sem)
    copy.start()
    copy.wait()


def second_body(first, bounds, left_at, right_at, table, ends, got, rest, before, other, mine, acc, old, sem):
    places = acc.shape[0]
    copy = pltpu.make_async_copy(before.at[pl.ds(first, places)], old, sem)
    copy.start()
    acc[...] = jnp.zeros(acc.shape, acc.dtype)
    contract(bounds, left_at, right_at, table, ends, flatten(got), flatten(rest), acc, first)
    copy.wait()
    for half, out in enumerate((other, mine)):
        span = pl.ds(half * (places // 2), places // 2)
        out[...] = acc[span] + old[span]


def load_body(first, bounds, left_at, right_at, table, ends, got, rest, before, other, mine, amp, acc, old, sems):
    cap = got.shape[1] - rest.shape[1]
    copy = pltpu.make_async_copy(got.at[:, pl.ds(0, cap)], amp.at[:, pl.ds(0, cap)], sems.at[1])
    copy.start()
    copy.wait()
    second_body(
        first, bounds, left_at, right_at, table, ends, amp, rest, before, other, mine, acc, old, sems.at[0]
    )


def group_table(order, start, stop, slots):
    rows = start.shape[0]
    at = order[:, None] == jnp.arange(rows)[None, :]

    def in_order(values):
        return jnp.sum(jnp.where(at, values[None, :], 0), axis=1)

    start, stop = in_order(start), in_order(stop)
    size = (stop - start) // GROUP
    end = jnp.sum(jnp.where(jnp.arange(rows)[:, None] >= jnp.arange(rows)[None, :], size[None, :], 0), axis=1)
    limit = rows * (slots // GROUP) + 2 * UNROLL
    number = jnp.arange(limit, dtype=jnp.int32)[:, None]
    passed = number >= end[None, :]
    place = jnp.minimum(jnp.sum(passed.astype(jnp.int32), axis=1), rows - 1)
    opened = jnp.max(jnp.where(passed, end[None, :], 0), axis=1)
    mine = place[:, None] == jnp.arange(rows)[None, :]

    def of_place(values):
        return jnp.sum(jnp.where(mine, values[None, :], 0), axis=1)

    base = of_place(start) + (number[:, 0] - opened) * GROUP
    base = jnp.where(number[:, 0] < end[-1], base, slots)
    table = jnp.stack([of_place(order), base, place]).astype(jnp.int32)
    ends = jnp.stack([order, stop, stop - start]).astype(jnp.int32)
    return end.astype(jnp.int32), table, ends


def body(amp_tiles, int_tiles, requests, tri_amp, tri_int, tri_count):
    wanted = requests[0, 0]
    peers, kinds, cap = wanted.shape
    rows, slots = tri_amp.shape[0], tri_amp.shape[2]
    tile = amp_tiles.shape[1:]
    cut = cap // 2
    red = lax.axis_size("red")
    share = rows // red
    steps = red // 2
    me = lax.axis_index("red")

    wanted, me = lax.optimization_barrier((wanted, me))
    asked = lax.all_to_all(wanted.reshape(peers, kinds * cap), "own", split_axis=0, concat_axis=0, tiled=True)
    first_list = tuple((0, s) for s in range(cap)) + tuple((1, s) for s in range(cut))
    second_list = tuple((1, s) for s in range(cut, cap))
    asked, me = lax.optimization_barrier((asked, me))
    stores = tuple(pltpu.with_memory_space_constraint(store, pltpu.VMEM) for store in (amp_tiles, int_tiles))
    send_first, send_second = pack((first_list, second_list), asked, stores)
    got_first = lax.all_to_all(send_first, "own", split_axis=0, concat_axis=0, tiled=True)
    got_first, send_second, tri_amp, tri_int, tri_count, me = lax.optimization_barrier(
        (got_first, send_second, tri_amp, tri_int, tri_count, me)
    )
    got_second = lax.all_to_all(send_second, "own", split_axis=0, concat_axis=0, tiled=True)

    amp_pos, int_pos = tri_amp[:, 0], tri_int[:, 0]
    count = tri_count[:, 0]
    alive = lax.broadcasted_iota(jnp.int32, (rows, slots), 1) < count[:, None]
    is_low = int_pos % cap < cut
    key = jnp.where(alive, jnp.where(is_low, 0, 1), 2)
    code = lax.sort((key * peers * cap + amp_pos) * peers * cap + int_pos, dimension=1)
    low = jnp.sum((alive & is_low).astype(jnp.int32), axis=1)
    amp_pos = (code // (peers * cap)) % (peers * cap)
    int_pos = code % (peers * cap)
    pad = ((0, 0), (0, GROUP))
    width = cap + cut
    holder, slot = int_pos // cap, int_pos % cap
    left_at = jnp.pad((amp_pos // cap) * width + amp_pos % cap, pad)
    right_at = jnp.where(slot < cut, holder * width + cap + slot, holder * (cap - cut) + slot - cut)
    right_at = jnp.pad(jnp.where(code < 2 * (peers * cap) ** 2, right_at, 0), pad)

    place = jnp.arange(rows, dtype=jnp.int32)
    step, side = place // (2 * share), (place // share) % 2
    order = (((me // 2 + step) % steps) * 2 + jnp.where(side == 0, 1 - me % 2, me % 2)) * share + place % share
    first_end, first_table, first_ends = group_table(order, jnp.zeros_like(low), low, slots)
    second_end, second_table, second_ends = group_table(order, low, count, slots)
    first_bounds = jnp.pad(first_end[rows - 1 :], (1, 0))
    second_bounds = jnp.pad(second_end[2 * share - 1 :: 2 * share], (1, 0))

    smem = pl.BlockSpec(memory_space=pltpu.SMEM)
    vmem = pl.BlockSpec(memory_space=pltpu.VMEM)
    params = pltpu.CompilerParams(vmem_limit_bytes=24 * 2**20)
    before = pl.pallas_call(
        first_body,
        in_specs=[smem] * 5 + [vmem],
        out_specs=pl.BlockSpec(memory_space=pltpu.HBM),
        out_shape=pltpu.HBM((rows,) + tile, jnp.float32),
        scratch_shapes=[pltpu.VMEM((rows,) + tile, jnp.float32), pltpu.SemaphoreType.DMA(())],
        compiler_params=params,
    )(first_bounds, left_at, right_at, first_table, first_ends, got_first)

    before = pltpu.with_memory_space_constraint(before, pltpu.HBM)

    def second(step, amp=None):
        half = jax.ShapeDtypeStruct((share,) + tile, jnp.float32)
        load = amp is None
        sems = pltpu.SemaphoreType.DMA((2,)) if load else pltpu.SemaphoreType.DMA(())
        hbm = pl.BlockSpec(memory_space=pltpu.HBM)
        return pl.pallas_call(
            functools.partial(load_body if load else second_body, step * 2 * share),
            in_specs=[smem] * 5 + [hbm if load else vmem, vmem, hbm],
            out_specs=[vmem] * (3 if load else 2),
            out_shape=[half, half] + ([jax.ShapeDtypeStruct(got_first.shape, got_first.dtype)] if load else []),
            scratch_shapes=[pltpu.VMEM((2 * share,) + tile, jnp.float32)] * 2 + [sems],
            compiler_params=params,
        )(
            second_bounds, left_at, right_at, second_table, second_ends, got_hbm if load else amp, got_second, before
        )

    got_hbm = pltpu.with_memory_space_constraint(got_first, pltpu.HBM)
    held = []
    swap = [(i, i ^ 1) for i in range(red)]

    def met(step, spans=(slice(None),), extra=0.0):
        other, mine, *amp = second(step, *held)
        held.extend(amp)
        theirs = lax.ppermute(other, "red", swap)
        return [mine[span] + theirs[span] + extra for span in spans]

    def send(value, distance):
        return lax.ppermute(value, "red", [(i, ((i // 2 + distance) % steps) * 2 + i % 2) for i in range(red)])

    half = share // 2
    far_low, far_high = met(2, (slice(0, half), slice(half, share)))
    from_left = send(far_low, 1)
    from_right = send(far_high, -1)
    still = ((0, 0), (0, 0))
    (right,) = met(1, extra=jnp.pad(from_left, ((0, share - half), *still)))
    from_left = send(right, 1)
    (left,) = met(3, extra=jnp.pad(from_right, ((half, 0), *still)))
    from_right = send(left, -1)
    return met(0)[0] + from_left + from_right


def solution(mesh):
    placed = (
        P(("own", "red"), None, None),
        P(("own", "red"), None, None),
        P("own", "red", None, None, None),
        P("own", "red", None),
        P("own", "red", None),
        P("own", "red"),
    )

    return jax.shard_map(body, mesh=mesh, in_specs=placed, out_specs=P(("own", "red"), None, None), check_vma=False)
```

```python
import functools

import jax
import jax.numpy as jnp
from jax import lax
from jax.experimental import pallas as pl
from jax.experimental.pallas import tpu as pltpu
from jax.sharding import PartitionSpec as P

GROUP = 8
UNROLL = 4
PACK_STEPS = 8
PARTS = 4


def copy_parts(pairs, sems):
    copies = []
    for number, (source, target) in enumerate(pairs):
        size = source.shape[0] // PARTS
        for i in range(PARTS):
            span = pl.ds(i * size, size)
            copies.append(pltpu.make_async_copy(source.at[span], target.at[span], sems.at[number * PARTS + i]))
    for copy in copies:
        copy.start()
    for copy in copies:
        copy.wait()


def pack_body(lists, asked, first_store, second_store, first_out, second_out, first_held, second_held, sems):
    stores, outs = (first_held, second_held), (first_out, second_out)

    @pl.when(pl.program_id(0) == 0)
    def _():
        copy_parts(((first_store, first_held), (second_store, second_held)), sems)

    cap = asked.shape[1] // 2
    last = stores[0].shape[0] - 1
    peers = outs[0].shape[0]
    first = pl.program_id(0) * peers
    for peer in range(peers):
        for out, picks in zip(outs, lists):
            for pos, (kind, slot) in enumerate(picks):
                tile = jnp.clip(asked[first + peer, kind * cap + slot], 0, last)
                out[peer, pos] = stores[kind][tile]


def pack(lists, asked, stores):
    peers = asked.shape[0]
    tile = stores[0].shape[1:]
    whole = pl.BlockSpec(memory_space=pltpu.HBM)
    return pl.pallas_call(
        functools.partial(pack_body, lists),
        grid=(PACK_STEPS,),
        in_specs=[pl.BlockSpec(memory_space=pltpu.SMEM), whole, whole],
        out_specs=[
            pl.BlockSpec((peers // PACK_STEPS, len(picks)) + tile, lambda i: (i, 0, 0, 0)) for picks in lists
        ],
        out_shape=[jax.ShapeDtypeStruct((peers, len(picks)) + tile, stores[0].dtype) for picks in lists],
        scratch_shapes=[pltpu.VMEM(store.shape, store.dtype) for store in stores]
        + [pltpu.SemaphoreType.DMA((2 * PARTS,))],
        compiler_params=pltpu.CompilerParams(vmem_limit_bytes=24 * 2**20),
    )(asked, *stores)


def group_dot(lefts, rights):
    return lax.dot_general(
        jnp.concatenate(lefts, axis=1),
        jnp.concatenate(rights, axis=1),
        (((1,), (1,)), ((), ())),
        preferred_element_type=jnp.float32,
    )


def contract(bounds, left_at, right_at, table, ends, left, right, acc, first, zero):
    places = acc.shape[0]
    begin = bounds[first - 1] if first else 0
    finish = bounds[first + places - 1]

    def full_step(i, carry):
        sums = []
        for u in range(UNROLL):
            g = begin + i * UNROLL + u
            row, base = table[0, g], table[1, g]
            lefts = [left[left_at[row, base + j]] for j in range(GROUP)]
            rights = [right[right_at[row, base + j]] for j in range(GROUP)]
            sums.append(group_dot(lefts, rights))
        for u in range(UNROLL):
            g = begin + i * UNROLL + u
            place = jnp.minimum(table[2, g] - first, places - 1)
            acc[place] = acc[place] + jnp.where(g < finish, sums[u], 0.0)
        return carry

    lax.fori_loop(0, (finish - begin + UNROLL - 1) // UNROLL, full_step, 0)

    def rest_step(i, carry):
        sums = []
        for u in range(UNROLL):
            place = first + i * UNROLL + u
            row, stop = ends[0, place], ends[1, place]
            base = stop - ends[2, place] % GROUP
            lefts, rights = [], []
            for j in range(GROUP):
                lefts.append(left[jnp.where(base + j < stop, left_at[row, base + j], zero)])
                rights.append(right[right_at[row, base + j]])
            sums.append(group_dot(lefts, rights))
        for u in range(UNROLL):
            place = i * UNROLL + u
            acc[place] = acc[place] + sums[u]
        return carry

    lax.fori_loop(0, places // UNROLL, rest_step, 0)


def flatten(ref):
    return ref.reshape((ref.shape[0] * ref.shape[1],) + ref.shape[2:])


def first_body(bounds, left_at, right_at, table, ends, got, out, acc, buf, sems):
    holders, width = got.shape[0], got.shape[1]
    acc[...] = jnp.zeros(acc.shape, acc.dtype)
    copy_parts(((got, buf.at[pl.ds(0, holders)]),), sems)
    buf[holders, 0] = jnp.zeros(buf.shape[2:], buf.dtype)
    flat = flatten(buf)
    contract(bounds, left_at, right_at, table, ends, flat, flat, acc, 0, holders * width)
    copy_parts(((acc, out),), sems)


def second_body(first, bounds, left_at, right_at, table, ends, got, rest, before, other, mine, acc, old, sem):
    places = acc.shape[0]
    copy = pltpu.make_async_copy(before.at[pl.ds(first, places)], old, sem)
    copy.start()
    acc[...] = jnp.zeros(acc.shape, acc.dtype)
    contract(bounds, left_at, right_at, table, ends, flatten(got), flatten(rest), acc, first, got.shape[1] - rest.shape[1])
    copy.wait()
    for half, out in enumerate((other, mine)):
        span = pl.ds(half * (places // 2), places // 2)
        out[...] = acc[span] + old[span]


def load_body(first, bounds, left_at, right_at, table, ends, got, rest, before, other, mine, amp, acc, old, sems):
    cap = got.shape[1] - rest.shape[1]
    copy_parts(((got.at[:, pl.ds(0, cap)], amp.at[:, pl.ds(0, cap)]),), sems)
    amp[0, cap] = jnp.zeros(amp.shape[2:], amp.dtype)
    second_body(
        first, bounds, left_at, right_at, table, ends, amp, rest, before, other, mine, acc, old, sems.at[PARTS]
    )


def group_table(order, start, stop, slots):
    rows = start.shape[0]
    at = order[:, None] == jnp.arange(rows)[None, :]

    def in_order(values):
        return jnp.sum(jnp.where(at, values[None, :], 0), axis=1)

    start, stop = in_order(start), in_order(stop)
    size = (stop - start) // GROUP
    end = jnp.sum(jnp.where(jnp.arange(rows)[:, None] >= jnp.arange(rows)[None, :], size[None, :], 0), axis=1)
    limit = rows * (slots // GROUP) + 2 * UNROLL
    number = jnp.arange(limit, dtype=jnp.int32)[:, None]
    passed = number >= end[None, :]
    place = jnp.minimum(jnp.sum(passed.astype(jnp.int32), axis=1), rows - 1)
    opened = jnp.max(jnp.where(passed, end[None, :], 0), axis=1)
    mine = place[:, None] == jnp.arange(rows)[None, :]

    def of_place(values):
        return jnp.sum(jnp.where(mine, values[None, :], 0), axis=1)

    base = of_place(start) + (number[:, 0] - opened) * GROUP
    base = jnp.where(number[:, 0] < end[-1], base, slots)
    table = jnp.stack([of_place(order), base, place]).astype(jnp.int32)
    ends = jnp.stack([order, stop, stop - start]).astype(jnp.int32)
    return end.astype(jnp.int32), table, ends


def body(amp_tiles, int_tiles, requests, tri_amp, tri_int, tri_count):
    wanted = requests[0, 0]
    peers, kinds, cap = wanted.shape
    rows, slots = tri_amp.shape[0], tri_amp.shape[2]
    tile = amp_tiles.shape[1:]
    cut = cap // 2
    red = lax.axis_size("red")
    share = rows // red
    steps = red // 2
    me = lax.axis_index("red")

    wanted, me = lax.optimization_barrier((wanted, me))
    asked = lax.all_to_all(wanted.reshape(peers, kinds * cap), "own", split_axis=0, concat_axis=0, tiled=True)
    first_list = tuple((0, s) for s in range(cap)) + tuple((1, s) for s in range(cut))
    second_list = tuple((1, s) for s in range(cut, cap))
    asked, me = lax.optimization_barrier((asked, me))
    stores = tuple(pltpu.with_memory_space_constraint(store, pltpu.HBM) for store in (amp_tiles, int_tiles))
    send_first, send_second = pack((first_list, second_list), asked, stores)
    got_first = lax.all_to_all(send_first, "own", split_axis=0, concat_axis=0, tiled=True)
    got_first, send_second, tri_amp, tri_int, tri_count, me = lax.optimization_barrier(
        (got_first, send_second, tri_amp, tri_int, tri_count, me)
    )
    got_second = lax.all_to_all(send_second, "own", split_axis=0, concat_axis=0, tiled=True)

    amp_pos, int_pos = tri_amp[:, 0], tri_int[:, 0]
    count = tri_count[:, 0]
    alive = lax.broadcasted_iota(jnp.int32, (rows, slots), 1) < count[:, None]
    is_low = int_pos % cap < cut
    key = jnp.where(alive, jnp.where(is_low, 0, 1), 2)
    code = lax.sort((key * peers * cap + amp_pos) * peers * cap + int_pos, dimension=1)
    low = jnp.sum((alive & is_low).astype(jnp.int32), axis=1)
    amp_pos = (code // (peers * cap)) % (peers * cap)
    int_pos = code % (peers * cap)
    pad = ((0, 0), (0, GROUP))
    width = cap + cut
    holder, slot = int_pos // cap, int_pos % cap
    left_at = jnp.pad((amp_pos // cap) * width + amp_pos % cap, pad)
    right_at = jnp.where(slot < cut, holder * width + cap + slot, holder * (cap - cut) + slot - cut)
    right_at = jnp.pad(jnp.where(code < 2 * (peers * cap) ** 2, right_at, 0), pad)

    place = jnp.arange(rows, dtype=jnp.int32)
    step, side = place // (2 * share), (place // share) % 2
    order = (((me // 2 + step) % steps) * 2 + jnp.where(side == 0, 1 - me % 2, me % 2)) * share + place % share
    first_bounds, first_table, first_ends = group_table(order, jnp.zeros_like(low), low, slots)
    second_bounds, second_table, second_ends = group_table(order, low, count, slots)

    smem = pl.BlockSpec(memory_space=pltpu.SMEM)
    vmem = pl.BlockSpec(memory_space=pltpu.VMEM)
    params = pltpu.CompilerParams(vmem_limit_bytes=24 * 2**20)
    hbm = pl.BlockSpec(memory_space=pltpu.HBM)
    got_hbm = pltpu.with_memory_space_constraint(got_first, pltpu.HBM)
    before = pl.pallas_call(
        first_body,
        in_specs=[smem] * 5 + [hbm],
        out_specs=hbm,
        out_shape=pltpu.HBM((rows,) + tile, jnp.float32),
        scratch_shapes=[
            pltpu.VMEM((rows,) + tile, jnp.float32),
            pltpu.VMEM((peers + 1, width) + tile, got_first.dtype),
            pltpu.SemaphoreType.DMA((PARTS,)),
        ],
        compiler_params=params,
    )(first_bounds, left_at, right_at, first_table, first_ends, got_hbm)

    before = pltpu.with_memory_space_constraint(before, pltpu.HBM)

    def second(step, amp=None):
        half = jax.ShapeDtypeStruct((share,) + tile, jnp.float32)
        load = amp is None
        sems = pltpu.SemaphoreType.DMA((PARTS + 1,)) if load else pltpu.SemaphoreType.DMA(())
        return pl.pallas_call(
            functools.partial(load_body if load else second_body, step * 2 * share),
            in_specs=[smem] * 5 + [hbm if load else vmem, vmem, hbm],
            out_specs=[vmem] * (3 if load else 2),
            out_shape=[half, half] + ([jax.ShapeDtypeStruct(got_first.shape, got_first.dtype)] if load else []),
            scratch_shapes=[pltpu.VMEM((2 * share,) + tile, jnp.float32)] * 2 + [sems],
            compiler_params=params,
        )(
            second_bounds, left_at, right_at, second_table, second_ends, got_hbm if load else amp, got_second, before
        )

    held = []
    swap = [(i, i ^ 1) for i in range(red)]

    def met(step, spans=(slice(None),), extra=0.0):
        other, mine, *amp = second(step, *held)
        held.extend(amp)
        theirs = lax.ppermute(other, "red", swap)
        return [mine[span] + theirs[span] + extra for span in spans]

    def send(value, distance):
        return lax.ppermute(value, "red", [(i, ((i // 2 + distance) % steps) * 2 + i % 2) for i in range(red)])

    half = share // 2
    far_low, far_high = met(2, (slice(0, half), slice(half, share)))
    from_left = send(far_low, 1)
    from_right = send(far_high, -1)
    still = ((0, 0), (0, 0))
    (right,) = met(1, extra=jnp.pad(from_left, ((0, share - half), *still)))
    from_left = send(right, 1)
    (left,) = met(3, extra=jnp.pad(from_right, ((half, 0), *still)))
    from_right = send(left, -1)
    return met(0)[0] + from_left + from_right


def solution(mesh):
    placed = (
        P(("own", "red"), None, None),
        P(("own", "red"), None, None),
        P("own", "red", None, None, None),
        P("own", "red", None),
        P("own", "red", None),
        P("own", "red"),
    )

    return jax.shard_map(body, mesh=mesh, in_specs=placed, out_specs=P(("own", "red"), None, None), check_vma=False)
```

```python
import functools

import jax
import jax.numpy as jnp
from jax import lax
from jax.experimental import pallas as pl
from jax.experimental.pallas import tpu as pltpu
from jax.sharding import PartitionSpec as P

GROUP = 8
UNROLL = 4
PACK_STEPS = 8
PARTS = 4


def copy_parts(pairs, sems):
    copies = []
    for number, (source, target) in enumerate(pairs):
        size = source.shape[0] // PARTS
        for i in range(PARTS):
            span = pl.ds(i * size, size)
            copies.append(pltpu.make_async_copy(source.at[span], target.at[span], sems.at[number * PARTS + i]))
    for copy in copies:
        copy.start()
    for copy in copies:
        copy.wait()


def pack_body(lists, asked, first_store, second_store, first_out, second_out, first_held, second_held, sems):
    stores, outs = (first_held, second_held), (first_out, second_out)

    @pl.when(pl.program_id(0) == 0)
    def _():
        copy_parts(((first_store, first_held), (second_store, second_held)), sems)

    cap = asked.shape[1] // 2
    last = stores[0].shape[0] - 1
    peers = outs[0].shape[0]
    first = pl.program_id(0) * peers
    for peer in range(peers):
        for out, picks in zip(outs, lists):
            for pos, (kind, slot) in enumerate(picks):
                tile = jnp.clip(asked[first + peer, kind * cap + slot], 0, last)
                out[peer, pos] = stores[kind][tile]


def pack(lists, asked, stores):
    peers = asked.shape[0]
    tile = stores[0].shape[1:]
    whole = pl.BlockSpec(memory_space=pltpu.HBM)
    return pl.pallas_call(
        functools.partial(pack_body, lists),
        grid=(PACK_STEPS,),
        in_specs=[pl.BlockSpec(memory_space=pltpu.SMEM), whole, whole],
        out_specs=[
            pl.BlockSpec((peers // PACK_STEPS, len(picks)) + tile, lambda i: (i, 0, 0, 0)) for picks in lists
        ],
        out_shape=[
            jax.ShapeDtypeStruct((peers, len(lists[0])) + tile, stores[0].dtype),
            pltpu.HBM((peers, len(lists[1])) + tile, stores[0].dtype),
        ],
        scratch_shapes=[pltpu.VMEM(store.shape, store.dtype) for store in stores]
        + [pltpu.SemaphoreType.DMA((2 * PARTS,))],
        compiler_params=pltpu.CompilerParams(vmem_limit_bytes=24 * 2**20),
    )(asked, *stores)


def group_dot(lefts, rights):
    return lax.dot_general(
        jnp.concatenate(lefts, axis=1),
        jnp.concatenate(rights, axis=1),
        (((1,), (1,)), ((), ())),
        preferred_element_type=jnp.float32,
    )


def contract(bounds, left_at, right_at, table, ends, left, right, acc, first, zero):
    places = acc.shape[0]
    begin = bounds[first - 1] if first else 0
    finish = bounds[first + places - 1]

    def full_step(i, carry):
        sums = []
        for u in range(UNROLL):
            g = begin + i * UNROLL + u
            row, base = table[0, g], table[1, g]
            lefts = [left[left_at[row, base + j]] for j in range(GROUP)]
            rights = [right[right_at[row, base + j]] for j in range(GROUP)]
            sums.append(group_dot(lefts, rights))
        for u in range(UNROLL):
            g = begin + i * UNROLL + u
            place = jnp.minimum(table[2, g] - first, places - 1)
            acc[place] = acc[place] + jnp.where(g < finish, sums[u], 0.0)
        return carry

    lax.fori_loop(0, (finish - begin + UNROLL - 1) // UNROLL, full_step, 0)

    def rest_step(i, carry):
        sums = []
        for u in range(UNROLL):
            place = first + i * UNROLL + u
            row, stop = ends[0, place], ends[1, place]
            base = stop - ends[2, place] % GROUP
            lefts, rights = [], []
            for j in range(GROUP):
                lefts.append(left[jnp.where(base + j < stop, left_at[row, base + j], zero)])
                rights.append(right[right_at[row, base + j]])
            sums.append(group_dot(lefts, rights))
        for u in range(UNROLL):
            place = i * UNROLL + u
            acc[place] = acc[place] + sums[u]
        return carry

    lax.fori_loop(0, places // UNROLL, rest_step, 0)


def flatten(ref):
    return ref.reshape((ref.shape[0] * ref.shape[1],) + ref.shape[2:])


def first_body(bounds, left_at, right_at, table, ends, got, out, acc, buf, sems):
    holders, width = got.shape[0], got.shape[1]
    acc[...] = jnp.zeros(acc.shape, acc.dtype)
    copy_parts(((got, buf.at[pl.ds(0, holders)]),), sems)
    buf[holders, 0] = jnp.zeros(buf.shape[2:], buf.dtype)
    flat = flatten(buf)
    contract(bounds, left_at, right_at, table, ends, flat, flat, acc, 0, holders * width)
    copy_parts(((acc, out),), sems)


def second_body(first, bounds, left_at, right_at, table, ends, got, rest, before, other, mine, acc, old, sem):
    places = acc.shape[0]
    copy = pltpu.make_async_copy(before.at[pl.ds(first, places)], old, sem)
    copy.start()
    acc[...] = jnp.zeros(acc.shape, acc.dtype)
    contract(bounds, left_at, right_at, table, ends, flatten(got), flatten(rest), acc, first, got.shape[1] - rest.shape[1])
    copy.wait()
    for half, out in enumerate((other, mine)):
        span = pl.ds(half * (places // 2), places // 2)
        out[...] = acc[span] + old[span]


def load_body(first, bounds, left_at, right_at, table, ends, got, rest, before, other, mine, amp, acc, old, sems):
    cap = got.shape[1] - rest.shape[1]
    copy_parts(((got.at[:, pl.ds(0, cap)], amp.at[:, pl.ds(0, cap)]),), sems)
    amp[0, cap] = jnp.zeros(amp.shape[2:], amp.dtype)
    second_body(
        first, bounds, left_at, right_at, table, ends, amp, rest, before, other, mine, acc, old, sems.at[PARTS]
    )


def group_table(order, start, stop, slots):
    rows = start.shape[0]
    at = order[:, None] == jnp.arange(rows)[None, :]

    def in_order(values):
        return jnp.sum(jnp.where(at, values[None, :], 0), axis=1)

    start, stop = in_order(start), in_order(stop)
    size = (stop - start) // GROUP
    end = jnp.sum(jnp.where(jnp.arange(rows)[:, None] >= jnp.arange(rows)[None, :], size[None, :], 0), axis=1)
    limit = rows * (slots // GROUP) + 2 * UNROLL
    number = jnp.arange(limit, dtype=jnp.int32)[:, None]
    passed = number >= end[None, :]
    place = jnp.minimum(jnp.sum(passed.astype(jnp.int32), axis=1), rows - 1)
    opened = jnp.max(jnp.where(passed, end[None, :], 0), axis=1)
    mine = place[:, None] == jnp.arange(rows)[None, :]

    def of_place(values):
        return jnp.sum(jnp.where(mine, values[None, :], 0), axis=1)

    base = of_place(start) + (number[:, 0] - opened) * GROUP
    base = jnp.where(number[:, 0] < end[-1], base, slots)
    table = jnp.stack([of_place(order), base, place]).astype(jnp.int32)
    ends = jnp.stack([order, stop, stop - start]).astype(jnp.int32)
    return end.astype(jnp.int32), table, ends


def body(amp_tiles, int_tiles, requests, tri_amp, tri_int, tri_count):
    wanted = requests[0, 0]
    peers, kinds, cap = wanted.shape
    rows, slots = tri_amp.shape[0], tri_amp.shape[2]
    tile = amp_tiles.shape[1:]
    cut = cap // 2
    red = lax.axis_size("red")
    share = rows // red
    steps = red // 2
    me = lax.axis_index("red")

    wanted, me = lax.optimization_barrier((wanted, me))
    asked = lax.all_to_all(wanted.reshape(peers, kinds * cap), "own", split_axis=0, concat_axis=0, tiled=True)
    first_list = tuple((0, s) for s in range(cap)) + tuple((1, s) for s in range(cut))
    second_list = tuple((1, s) for s in range(cut, cap))
    asked, me = lax.optimization_barrier((asked, me))
    stores = tuple(pltpu.with_memory_space_constraint(store, pltpu.HBM) for store in (amp_tiles, int_tiles))
    send_first, send_second = pack((first_list, second_list), asked, stores)
    got_first = lax.all_to_all(send_first, "own", split_axis=0, concat_axis=0, tiled=True)
    got_first, send_second, tri_amp, tri_int, tri_count, me = lax.optimization_barrier(
        (got_first, send_second, tri_amp, tri_int, tri_count, me)
    )
    got_second = lax.all_to_all(send_second, "own", split_axis=0, concat_axis=0, tiled=True)

    amp_pos, int_pos = tri_amp[:, 0], tri_int[:, 0]
    count = tri_count[:, 0]
    alive = lax.broadcasted_iota(jnp.int32, (rows, slots), 1) < count[:, None]
    is_low = int_pos % cap < cut
    key = jnp.where(alive, jnp.where(is_low, 0, 1), 2)
    code = lax.sort((key * peers * cap + amp_pos) * peers * cap + int_pos, dimension=1)
    low = jnp.sum((alive & is_low).astype(jnp.int32), axis=1)
    amp_pos = (code // (peers * cap)) % (peers * cap)
    int_pos = code % (peers * cap)
    pad = ((0, 0), (0, GROUP))
    width = cap + cut
    holder, slot = int_pos // cap, int_pos % cap
    left_at = jnp.pad((amp_pos // cap) * width + amp_pos % cap, pad)
    right_at = jnp.where(slot < cut, holder * width + cap + slot, holder * (cap - cut) + slot - cut)
    right_at = jnp.pad(jnp.where(code < 2 * (peers * cap) ** 2, right_at, 0), pad)

    place = jnp.arange(rows, dtype=jnp.int32)
    step, side = place // (2 * share), (place // share) % 2
    order = (((me // 2 + step) % steps) * 2 + jnp.where(side == 0, 1 - me % 2, me % 2)) * share + place % share
    first_bounds, first_table, first_ends = group_table(order, jnp.zeros_like(low), low, slots)
    second_bounds, second_table, second_ends = group_table(order, low, count, slots)

    smem = pl.BlockSpec(memory_space=pltpu.SMEM)
    vmem = pl.BlockSpec(memory_space=pltpu.VMEM)
    params = pltpu.CompilerParams(vmem_limit_bytes=24 * 2**20)
    hbm = pl.BlockSpec(memory_space=pltpu.HBM)
    got_hbm = pltpu.with_memory_space_constraint(got_first, pltpu.HBM)
    before = pl.pallas_call(
        first_body,
        in_specs=[smem] * 5 + [hbm],
        out_specs=hbm,
        out_shape=pltpu.HBM((rows,) + tile, jnp.float32),
        scratch_shapes=[
            pltpu.VMEM((rows,) + tile, jnp.float32),
            pltpu.VMEM((peers + 1, width) + tile, got_first.dtype),
            pltpu.SemaphoreType.DMA((PARTS,)),
        ],
        compiler_params=params,
    )(first_bounds, left_at, right_at, first_table, first_ends, got_hbm)

    before = pltpu.with_memory_space_constraint(before, pltpu.HBM)

    def second(step, amp=None):
        half = jax.ShapeDtypeStruct((share,) + tile, jnp.float32)
        load = amp is None
        sems = pltpu.SemaphoreType.DMA((PARTS + 1,)) if load else pltpu.SemaphoreType.DMA(())
        return pl.pallas_call(
            functools.partial(load_body if load else second_body, step * 2 * share),
            in_specs=[smem] * 5 + [hbm if load else vmem, vmem, hbm],
            out_specs=[vmem] * (3 if load else 2),
            out_shape=[half, half] + ([jax.ShapeDtypeStruct(got_first.shape, got_first.dtype)] if load else []),
            scratch_shapes=[pltpu.VMEM((2 * share,) + tile, jnp.float32)] * 2 + [sems],
            compiler_params=params,
        )(
            second_bounds, left_at, right_at, second_table, second_ends, got_hbm if load else amp, got_second, before
        )

    held = []
    swap = [(i, i ^ 1) for i in range(red)]

    def met(step, spans=(slice(None),), extra=0.0):
        other, mine, *amp = second(step, *held)
        held.extend(amp)
        theirs = lax.ppermute(other, "red", swap)
        return [mine[span] + theirs[span] + extra for span in spans]

    def send(value, distance):
        return lax.ppermute(value, "red", [(i, ((i // 2 + distance) % steps) * 2 + i % 2) for i in range(red)])

    half = share // 2
    far_low, far_high = met(2, (slice(0, half), slice(half, share)))
    from_left = send(far_low, 1)
    from_right = send(far_high, -1)
    still = ((0, 0), (0, 0))
    (right,) = met(1, extra=jnp.pad(from_left, ((0, share - half), *still)))
    from_left = send(right, 1)
    (left,) = met(3, extra=jnp.pad(from_right, ((half, 0), *still)))
    from_right = send(left, -1)
    return met(0)[0] + from_left + from_right


def solution(mesh):
    placed = (
        P(("own", "red"), None, None),
        P(("own", "red"), None, None),
        P("own", "red", None, None, None),
        P("own", "red", None),
        P("own", "red", None),
        P("own", "red"),
    )

    return jax.shard_map(body, mesh=mesh, in_specs=placed, out_specs=P(("own", "red"), None, None), check_vma=False)
```
